128 devices in a mesh: seq: 16 (over z, y_lo, core), head: 8 (over x, y_hi).
Axes of the slice: x: 4, y: 4 (y_hi: 2, y_lo: 2; y = y_hi * 2 + y_lo), z: 4, core: 2. Of those that a mesh axis runs over, the one named last changes fastest.
Arguments:
- tokens: bfloat16 [128, 512, 1024], P('seq'), may hold values from -36 to 36
- lengths: int32 [128], P('seq'), may hold values from 1 to 512, 32768 in all
- attn_in: float32 [1024, 3, 1024], P(('seq', 'head')), may hold values from -0.4 to 0.4
- attn_out: float32 [1024, 1024], P(None, ('seq', 'head')), may hold values from -0.1875 to 0.1875
- mlp_in: float32 [1024, 4096], P(('seq', 'head')), may hold values from -0.1875 to 0.1875
- mlp_out: float32 [4096, 1024], P(None, ('seq', 'head')), may hold values from -0.09375 to 0.09375
- norm_gain: float32 [2, 1024], replicated, may hold values from 0.5 to 1.5
- norm_shift: float32 [2, 1024], replicated, may hold values from -3 to 3
Outputs:
- encoded: bfloat16 [128, 512, 1024], P('seq', 'head')
- key_cache: bfloat16 [128, 512, 1024], P('seq', None, 'head')
- value_cache: bfloat16 [128, 512, 1024], P('seq', None, 'head')
The draws below stay inside these ranges and needn't reach their ends.
Inputs may be any that keep to these rules, and one draw needn't show every extreme that they name: `lengths`: some prompt has exactly 512 tokens.
All inputs are finite; a program needn't handle non-finite values. No bound on the sum of `lengths` on one device may be relied on, other than what follows from the above.
Results may differ from the reference program's by a relative error of at most 0.02.
Values may be sent and summed in bfloat16 or wider, within the bound.
A program may use at most 128 MiB of HBM per device.

```python
import math
import jax
import jax.numpy as jnp
import numpy as np
from jax import lax

D = 1024
H = 16
FF = 4096
DH = 64
LEN = 512
PROMPTS = 128
N_HEAD = 8


def draw_tokens(key, part):
    keys = jax.random.split(key, 3)
    base = jnp.clip(jax.random.normal(keys[0], (PROMPTS, LEN, D), jnp.float32), -3.0, 3.0)
    row_scale = jnp.exp(jax.random.uniform(keys[1], (PROMPTS, LEN, 1), jnp.float32, math.log(0.4), math.log(4.0)))
    col_scale = jnp.exp(jax.random.uniform(keys[2], (1, 1, D), jnp.float32, math.log(0.3), math.log(3.0)))
    field = base * row_scale * col_scale
    return field.astype(jnp.bfloat16)


def draw_attn_in(key, part):
    keys = jax.random.split(key, 3)
    scale_factor = 1.0 / math.sqrt(D)
    query_part = jnp.clip(jax.random.normal(keys[0], (D, D), jnp.float32), -4.0, 4.0) * scale_factor
    key_part = jnp.clip(jax.random.normal(keys[1], (D, D), jnp.float32), -4.0, 4.0) * scale_factor
    value_part = jnp.clip(jax.random.normal(keys[2], (D, D), jnp.float32), -4.0, 4.0) * scale_factor
    return jnp.stack([query_part, key_part, value_part], axis=1)


def block_levels(rng, shape, cuts, low, high):
    level = 1.0
    for axis_at, blocks in cuts:
        draws = jax.random.uniform(jax.random.fold_in(jax.random.fold_in(rng, 6), axis_at), (blocks,), jnp.float32, low / len(cuts), high / len(cuts))
        level = level * jnp.repeat(jnp.exp(draws), shape[axis_at] // blocks).reshape((-1,) + (1,) * (len(shape) - 1 - axis_at))
    return level


def length_profile(amount, total, limit, skew):
    weights = [(1 << 20) // math.isqrt(rank ** skew) + 1 for rank in range(2, amount + 1)]
    surplus, given = total - limit - (amount - 1), [1] * (amount - 1)
    while surplus > 0:
        free = [i for i in range(amount - 1) if given[i] < limit]
        mass, budget = sum([weights[i] for i in free]), surplus
        for i in free:
            addition = min(limit - given[i], max(1, budget * weights[i] // mass), surplus)
            given[i] = given[i] + addition
            surplus = surplus - addition
    return np.array([limit] + given)


def uneven(own_key, number_of, total, most, skew):
    if number_of == 2:
        one = jax.random.randint(own_key, (), max(1, total - most), min(most, total - 1) + 1)
        return jnp.stack([one, total - one])
    sizes = jnp.asarray(length_profile(number_of, total, most, skew), jnp.int32)
    twos = (number_of - 1) // 2
    giver, taker = sizes[1:1 + 2 * twos:2], sizes[2:2 + 2 * twos:2]
    margin = jnp.minimum(giver - 1, most - taker)
    shifted = jax.random.randint(jax.random.fold_in(own_key, 1), (twos,), 0, 1 << 20) % (margin + 1)
    sizes = sizes.at[1:1 + 2 * twos:2].set(giver - shifted).at[2:2 + 2 * twos:2].set(taker + shifted)
    return sizes[jax.random.permutation(jax.random.fold_in(own_key, 2), number_of)]


def noise(stream_key, shape, deviation, bound, cuts=(), held_as=jnp.bfloat16):
    drawn = deviation * jax.random.normal(stream_key, shape, jnp.float32)
    if cuts:
        drawn = drawn * block_levels(stream_key, shape, cuts, -0.22, 0.18)
    return jnp.clip(drawn, -bound, bound).astype(held_as)


def setup_inputs(seed: int = 0) -> dict:
    seeds = jax.random.split(jax.random.key(seed), 9)
    return {
        "tokens": draw_tokens(jax.random.fold_in(seeds[8], 71), 0),
        "lengths": uneven(seeds[1], PROMPTS, PROMPTS * LEN // 2, LEN, 2).astype(jnp.int32),
        "attn_in": draw_attn_in(jax.random.fold_in(seeds[8], 71), 0),
        "attn_out": noise(seeds[3], (D, D), D ** -0.5, 0.1875, ((1, 128),), jnp.float32),
        "mlp_in": noise(seeds[4], (D, FF), D ** -0.5, 0.1875, ((0, 128),), jnp.float32),
        "mlp_out": noise(seeds[5], (FF, D), FF ** -0.5, 0.09375, ((1, 128),), jnp.float32),
        "norm_gain": jnp.clip(1.0 + 0.1 * jax.random.normal(seeds[6], (2, D), jnp.float32), 0.5, 1.5),
        "norm_shift": noise(seeds[7], (2, D), 0.5, 3.0, (), jnp.float32),
    }


EPSILON = 1e-05

def layer_norm(values, gain, shift):
    center = values - lax.optimization_barrier(jnp.mean(values, axis=-1, keepdims=True))
    spread = lax.optimization_barrier(jnp.mean(center * center, axis=-1, keepdims=True))
    return center * lax.rsqrt(spread + EPSILON) * gain + shift

def block_sum(left_side, right_side, blocks):
    block_cols = left_side.shape[1] // blocks
    summed = jnp.zeros((left_side.shape[0], right_side.shape[1]), jnp.float32)
    for block_index in range(blocks):
        lower = block_index * block_cols
        partial_sum = jnp.dot(left_side[:, lower:lower + block_cols], right_side[lower:lower + block_cols], preferred_element_type=jnp.float32)
        rounded = lax.optimization_barrier(partial_sum.astype(jnp.bfloat16))
        summed = summed + rounded.astype(jnp.float32)
    return summed

def reference(tokens, lengths, attn_in, attn_out, mlp_in, mlp_out, norm_gain, norm_shift):
    qkv_weight = attn_in.astype(jnp.bfloat16).reshape(D, 3 * D)
    proj_weight = attn_out.astype(jnp.bfloat16)
    up_weight = mlp_in.astype(jnp.bfloat16)
    down_weight = mlp_out.astype(jnp.bfloat16)
    scale_factor = 1.0 / math.sqrt(DH)
    positions = jnp.arange(LEN, dtype=jnp.int32)

    def encode_prompt(operands):
        prompt_tokens, prompt_length = operands
        inside = positions < prompt_length
        projected = jnp.dot(prompt_tokens, qkv_weight, preferred_element_type=jnp.float32).astype(jnp.bfloat16)
        projected = projected.reshape(LEN, 3, H, DH)
        queries = projected[:, 0].astype(jnp.float32)
        key_heads = projected[:, 1].astype(jnp.float32)
        value_heads = projected[:, 2].astype(jnp.float32)
        scores = jnp.einsum('qhd,khd->hqk', queries, key_heads) * scale_factor
        scores = jnp.where(inside[None, None, :], scores, -1e+30)
        row_peak = lax.optimization_barrier(jnp.max(scores, axis=-1, keepdims=True))
        raised = jnp.exp(scores - row_peak)
        weights = (raised / lax.optimization_barrier(jnp.sum(raised, axis=-1, keepdims=True))).astype(jnp.bfloat16)
        context = jnp.einsum('hqk,khd->qhd', weights.astype(jnp.float32), value_heads)
        context = context.astype(jnp.bfloat16).reshape(LEN, D)
        attended = block_sum(context, proj_weight, N_HEAD)
        normed = layer_norm(prompt_tokens.astype(jnp.float32) + attended, norm_gain[0], norm_shift[0]).astype(jnp.bfloat16)
        hidden = jax.nn.gelu(jnp.dot(normed, up_weight, preferred_element_type=jnp.float32), approximate=False).astype(jnp.bfloat16)
        mixed = block_sum(hidden, down_weight, N_HEAD)
        finished = layer_norm(normed.astype(jnp.float32) + mixed, norm_gain[1], norm_shift[1])
        row_mask = inside[:, None]
        encoded = jnp.where(row_mask, finished, 0.0).astype(jnp.bfloat16)
        key_rows = projected[:, 1].reshape(LEN, D)
        value_rows = projected[:, 2].reshape(LEN, D)
        key_cache = jnp.where(row_mask, key_rows, jnp.zeros_like(key_rows))
        value_cache = jnp.where(row_mask, value_rows, jnp.zeros_like(value_rows))
        return (encoded, key_cache, value_cache)
    encoded, key_cache, value_cache = lax.map(encode_prompt, (tokens, lengths))
    return (encoded, key_cache, value_cache)
```

```python
import math

import jax
import jax.numpy as jnp
from jax import lax
from jax.sharding import PartitionSpec as P

DH = 64


EPSILON = 1e-05


def layer_norm(values, gain, shift):
    center = values - jnp.mean(values, axis=-1, keepdims=True)
    spread = jnp.mean(center * center, axis=-1, keepdims=True)
    return center * lax.rsqrt(spread + EPSILON) * gain + shift


def regroup_weights(attn_in, attn_out, mlp_in, mlp_out, heads_axis):
    rows = attn_in.shape[0]
    model_width = attn_in.shape[2]
    hidden_width = mlp_in.shape[1]
    block_width = model_width // heads_axis
    hidden_block = hidden_width // heads_axis
    in_piece = attn_in.astype(jnp.bfloat16).reshape(rows, 3, heads_axis, block_width)
    in_piece = jnp.transpose(in_piece, (0, 2, 1, 3)).reshape(rows, heads_axis, 3 * block_width)
    up_piece = mlp_in.astype(jnp.bfloat16).reshape(rows, heads_axis, hidden_block)
    out_piece = attn_out.astype(jnp.bfloat16).T.reshape(rows, heads_axis, block_width)
    down_piece = mlp_out.astype(jnp.bfloat16).T.reshape(rows, heads_axis, hidden_block)
    packed = jnp.concatenate([in_piece, up_piece, out_piece, down_piece], axis=2)
    packed = lax.all_to_all(packed, "head", 1, 0, tiled=True)
    packed = packed.reshape(rows * heads_axis, packed.shape[2])
    whole = lax.all_gather(packed, "seq", axis=0, tiled=True)
    edges = [0, 3 * block_width, 3 * block_width + hidden_block,
             4 * block_width + hidden_block, 4 * block_width + 2 * hidden_block]
    qkv_weight = whole[:, edges[0]:edges[1]].reshape(-1, 3, block_width)
    up_weight = whole[:, edges[1]:edges[2]]
    proj_weight_t = whole[:, edges[2]:edges[3]]
    down_weight_t = whole[:, edges[3]:edges[4]]
    return qkv_weight, up_weight, proj_weight_t, down_weight_t


def shards(tokens, lengths, attn_in, attn_out, mlp_in, mlp_out, norm_gain, norm_shift):
    heads_axis = lax.axis_size("head")
    head_index = lax.axis_index("head")
    prompts = tokens.shape[0]
    seq_len = tokens.shape[1]
    model_width = tokens.shape[2]
    block_width = model_width // heads_axis
    local_heads = block_width // DH
    qkv_weight, up_weight, proj_weight_t, down_weight_t = regroup_weights(
        attn_in, attn_out, mlp_in, mlp_out, heads_axis)
    projected = jnp.einsum(
        "pld,dte->plte", tokens, qkv_weight, preferred_element_type=jnp.float32
    ).astype(jnp.bfloat16)
    positions = jnp.arange(seq_len, dtype=jnp.int32)
    inside = positions[None, :] < lengths[:, None]
    key_part = projected[:, :, 1]
    value_part = projected[:, :, 2]
    queries = projected[:, :, 0].reshape(prompts, seq_len, local_heads, DH)
    key_heads = key_part.reshape(prompts, seq_len, local_heads, DH)
    value_heads = value_part.reshape(prompts, seq_len, local_heads, DH)
    scores = jnp.einsum(
        "pqhd,pkhd->phqk", queries, key_heads, preferred_element_type=jnp.float32
    ) * (1.0 / math.sqrt(DH))
    scores = jnp.where(inside[:, None, None, :], scores, -1e30)
    row_peak = jnp.max(scores, axis=-1, keepdims=True)
    raised = jnp.exp(scores - row_peak)
    weights = (raised / jnp.sum(raised, axis=-1, keepdims=True)).astype(jnp.bfloat16)
    context = jnp.einsum(
        "phqk,pkhd->pqhd", weights, value_heads, preferred_element_type=jnp.float32
    )
    context = context.astype(jnp.bfloat16).reshape(prompts, seq_len, block_width)
    key_cache = jnp.where(inside[:, :, None], key_part, jnp.zeros_like(key_part))
    value_cache = jnp.where(inside[:, :, None], value_part, jnp.zeros_like(value_part))
    row_count = seq_len // heads_axis
    row_start = head_index * row_count
    attn_partial = jnp.einsum(
        "pld,ed->ple", context, proj_weight_t, preferred_element_type=jnp.float32
    )
    attn_total = lax.psum(attn_partial.astype(jnp.bfloat16), "head").astype(jnp.float32)
    normed = layer_norm(
        tokens.astype(jnp.float32) + attn_total, norm_gain[0], norm_shift[0]
    ).astype(jnp.bfloat16)
    hidden = jax.nn.gelu(
        jnp.einsum("pld,df->plf", normed, up_weight, preferred_element_type=jnp.float32),
        approximate=False,
    ).astype(jnp.bfloat16)
    mlp_partial = jnp.einsum("plf,ef->ple", hidden, down_weight_t, preferred_element_type=jnp.float32)
    mlp_rows = lax.psum_scatter(
        mlp_partial.astype(jnp.bfloat16), "head", scatter_dimension=1, tiled=True
    ).astype(jnp.float32)
    normed_rows = lax.dynamic_slice_in_dim(normed, row_start, row_count, 1)
    finished = layer_norm(normed_rows.astype(jnp.float32) + mlp_rows, norm_gain[1], norm_shift[1])
    inside_rows = lax.dynamic_slice_in_dim(inside, row_start, row_count, 1)
    encoded = jnp.where(inside_rows[:, :, None], finished, 0.0).astype(jnp.bfloat16)
    return (encoded, key_cache, value_cache)


def solution(mesh):
    in_specs = (
        P("seq", None, None),
        P("seq"),
        P(("seq", "head"), None, None),
        P(None, ("seq", "head")),
        P(("seq", "head"), None),
        P(None, ("seq", "head")),
        P(),
        P(),
    )
    out_specs = (P("seq", "head", None), P("seq", None, "head"), P("seq", None, "head"))
    return jax.shard_map(shards, mesh=mesh, in_specs=in_specs, out_specs=out_specs, check_vma=False)
```

```python
import math

import jax
import jax.numpy as jnp
from jax import lax
from jax.sharding import PartitionSpec as P

DH = 64


EPSILON = 1e-05


def layer_norm(values, gain, shift):
    center = values - jnp.mean(values, axis=-1, keepdims=True)
    spread = jnp.mean(center * center, axis=-1, keepdims=True)
    return center * lax.rsqrt(spread + EPSILON) * gain + shift


def regroup_weights(attn_in, attn_out, mlp_in, mlp_out, heads_axis):
    rows = attn_in.shape[0]
    model_width = attn_in.shape[2]
    hidden_width = mlp_in.shape[1]
    block_width = model_width // heads_axis
    hidden_block = hidden_width // heads_axis
    in_piece = attn_in.astype(jnp.bfloat16).reshape(rows, 3, heads_axis, block_width)
    in_piece = jnp.transpose(in_piece, (0, 2, 1, 3)).reshape(rows, heads_axis, 3 * block_width)
    up_piece = mlp_in.astype(jnp.bfloat16).reshape(rows, heads_axis, hidden_block)
    out_piece = attn_out.astype(jnp.bfloat16).T.reshape(rows, heads_axis, block_width)
    down_piece = mlp_out.astype(jnp.bfloat16).T.reshape(rows, heads_axis, hidden_block)
    packed = jnp.concatenate([in_piece, up_piece, out_piece, down_piece], axis=2)
    packed = lax.all_to_all(packed, "head", 1, 0, tiled=True)
    packed = packed.reshape(rows * heads_axis, packed.shape[2])
    whole = lax.all_gather(packed, "seq", axis=0, tiled=True)
    edges = [0, 3 * block_width, 3 * block_width + hidden_block,
             4 * block_width + hidden_block, 4 * block_width + 2 * hidden_block]
    qkv_weight = whole[:, edges[0]:edges[1]].reshape(-1, 3, block_width)
    up_weight = whole[:, edges[1]:edges[2]]
    proj_weight_t = whole[:, edges[2]:edges[3]]
    down_weight_t = whole[:, edges[3]:edges[4]]
    return qkv_weight, up_weight, proj_weight_t, down_weight_t


def shards(tokens, lengths, attn_in, attn_out, mlp_in, mlp_out, norm_gain, norm_shift):
    heads_axis = lax.axis_size("head")
    head_index = lax.axis_index("head")
    prompts = tokens.shape[0]
    seq_len = tokens.shape[1]
    model_width = tokens.shape[2]
    block_width = model_width // heads_axis
    local_heads = block_width // DH
    qkv_weight, up_weight, proj_weight_t, down_weight_t = regroup_weights(
        attn_in, attn_out, mlp_in, mlp_out, heads_axis)
    projected = jnp.einsum(
        "pld,dte->plte", tokens, qkv_weight, preferred_element_type=jnp.float32
    ).astype(jnp.bfloat16)
    positions = jnp.arange(seq_len, dtype=jnp.int32)
    inside = positions[None, :] < lengths[:, None]
    key_part = projected[:, :, 1]
    value_part = projected[:, :, 2]
    queries = projected[:, :, 0].reshape(prompts, seq_len, local_heads, DH)
    key_heads = key_part.reshape(prompts, seq_len, local_heads, DH)
    value_heads = value_part.reshape(prompts, seq_len, local_heads, DH)
    scores = jnp.einsum(
        "pqhd,pkhd->phqk", queries, key_heads, preferred_element_type=jnp.float32
    ) * (1.0 / math.sqrt(DH))
    scores = jnp.where(inside[:, None, None, :], scores, -1e30)
    row_peak = jnp.max(scores, axis=-1, keepdims=True)
    raised = jnp.exp(scores - row_peak)
    weights = (raised / jnp.sum(raised, axis=-1, keepdims=True)).astype(jnp.bfloat16)
    context = jnp.einsum(
        "phqk,pkhd->pqhd", weights, value_heads, preferred_element_type=jnp.float32
    )
    context = context.astype(jnp.bfloat16).reshape(prompts, seq_len, block_width)
    key_cache = jnp.where(inside[:, :, None], key_part, jnp.zeros_like(key_part))
    value_cache = jnp.where(inside[:, :, None], value_part, jnp.zeros_like(value_part))
    row_count = seq_len // heads_axis
    row_start = head_index * row_count
    attn_partial = jnp.einsum(
        "pld,ed->ple", context, proj_weight_t, preferred_element_type=jnp.float32
    )
    attn_rows = lax.psum_scatter(
        attn_partial.astype(jnp.bfloat16), "head", scatter_dimension=1, tiled=True
    ).astype(jnp.float32)
    token_rows = lax.dynamic_slice_in_dim(tokens, row_start, row_count, 1)
    normed_rows = layer_norm(
        token_rows.astype(jnp.float32) + attn_rows, norm_gain[0], norm_shift[0]
    ).astype(jnp.bfloat16)
    normed = lax.all_gather(normed_rows, "head", axis=1, tiled=True)
    hidden = jax.nn.gelu(
        jnp.einsum("pld,df->plf", normed, up_weight, preferred_element_type=jnp.float32),
        approximate=False,
    ).astype(jnp.bfloat16)
    mlp_partial = jnp.einsum("plf,ef->ple", hidden, down_weight_t, preferred_element_type=jnp.float32)
    mlp_rows = lax.psum_scatter(
        mlp_partial.astype(jnp.bfloat16), "head", scatter_dimension=1, tiled=True
    ).astype(jnp.float32)
    finished = layer_norm(normed_rows.astype(jnp.float32) + mlp_rows, norm_gain[1], norm_shift[1])
    inside_rows = lax.dynamic_slice_in_dim(inside, row_start, row_count, 1)
    encoded = jnp.where(inside_rows[:, :, None], finished, 0.0).astype(jnp.bfloat16)
    return (encoded, key_cache, value_cache)


def solution(mesh):
    in_specs = (
        P("seq", None, None),
        P("seq"),
        P(("seq", "head"), None, None),
        P(None, ("seq", "head")),
        P(("seq", "head"), None),
        P(None, ("seq", "head")),
        P(),
        P(),
    )
    out_specs = (P("seq", "head", None), P("seq", None, "head"), P("seq", None, "head"))
    return jax.shard_map(shards, mesh=mesh, in_specs=in_specs, out_specs=out_specs, check_vma=False)
```

```python
import math

import jax
import jax.numpy as jnp
from jax import lax
from jax.sharding import PartitionSpec as P

DH = 64


EPSILON = 1e-05


def layer_norm(values, gain, shift):
    center = values - jnp.mean(values, axis=-1, keepdims=True)
    spread = jnp.mean(center * center, axis=-1, keepdims=True)
    return center * lax.rsqrt(spread + EPSILON) * gain + shift


def regroup_weights(attn_in, attn_out, heads_axis):
    rows = attn_in.shape[0]
    model_width = attn_in.shape[2]
    block_width = model_width // heads_axis
    in_piece = attn_in.astype(jnp.bfloat16).reshape(rows, 3, heads_axis, block_width)
    in_piece = jnp.transpose(in_piece, (0, 2, 1, 3)).reshape(rows, heads_axis, 3 * block_width)
    out_piece = attn_out.astype(jnp.bfloat16).T.reshape(rows, heads_axis, block_width)
    packed = jnp.concatenate([in_piece, out_piece], axis=2)
    packed = lax.all_to_all(packed, "head", 1, 0, tiled=True)
    packed = packed.reshape(rows * heads_axis, packed.shape[2])
    whole = lax.all_gather(packed, "seq", axis=0, tiled=True)
    qkv_weight = whole[:, :3 * block_width].reshape(-1, 3, block_width)
    proj_weight_t = whole[:, 3 * block_width:]
    return qkv_weight, proj_weight_t


def gather_mlp(mlp_in, mlp_out):
    hidden_width = mlp_in.shape[1]
    packed = jnp.concatenate(
        [mlp_in.astype(jnp.bfloat16), mlp_out.astype(jnp.bfloat16).T], axis=1)
    packed = lax.all_gather(packed, "head", axis=0, tiled=True)
    whole = lax.all_gather(packed, "seq", axis=0, tiled=True)
    return whole[:, :hidden_width], whole[:, hidden_width:]


def shards(tokens, lengths, attn_in, attn_out, mlp_in, mlp_out, norm_gain, norm_shift):
    heads_axis = lax.axis_size("head")
    head_index = lax.axis_index("head")
    prompts = tokens.shape[0]
    seq_len = tokens.shape[1]
    model_width = tokens.shape[2]
    hidden_width = mlp_in.shape[1]
    block_width = model_width // heads_axis
    hidden_block = hidden_width // heads_axis
    local_heads = block_width // DH
    qkv_weight, proj_weight_t = regroup_weights(attn_in, attn_out, heads_axis)
    up_weight, down_weight_t = gather_mlp(mlp_in, mlp_out)
    projected = jnp.einsum(
        "pld,dte->plte", tokens, qkv_weight, preferred_element_type=jnp.float32
    ).astype(jnp.bfloat16)
    positions = jnp.arange(seq_len, dtype=jnp.int32)
    inside = positions[None, :] < lengths[:, None]
    key_part = projected[:, :, 1]
    value_part = projected[:, :, 2]
    queries = projected[:, :, 0].reshape(prompts, seq_len, local_heads, DH)
    key_heads = key_part.reshape(prompts, seq_len, local_heads, DH)
    value_heads = value_part.reshape(prompts, seq_len, local_heads, DH)
    scores = jnp.einsum(
        "pqhd,pkhd->phqk", queries, key_heads, preferred_element_type=jnp.float32
    ) * (1.0 / math.sqrt(DH))
    scores = jnp.where(inside[:, None, None, :], scores, -1e30)
    row_peak = jnp.max(scores, axis=-1, keepdims=True)
    raised = jnp.exp(scores - row_peak)
    weights = (raised / jnp.sum(raised, axis=-1, keepdims=True)).astype(jnp.bfloat16)
    context = jnp.einsum(
        "phqk,pkhd->pqhd", weights, value_heads, preferred_element_type=jnp.float32
    )
    context = context.astype(jnp.bfloat16).reshape(prompts, seq_len, block_width)
    key_cache = jnp.where(inside[:, :, None], key_part, jnp.zeros_like(key_part))
    value_cache = jnp.where(inside[:, :, None], value_part, jnp.zeros_like(value_part))
    row_count = seq_len // heads_axis
    row_start = head_index * row_count
    attn_partial = jnp.einsum(
        "pld,ed->ple", context, proj_weight_t, preferred_element_type=jnp.float32
    ).astype(jnp.bfloat16)
    attn_blocks = lax.all_to_all(
        attn_partial.reshape(prompts, heads_axis, row_count, model_width), "head", 1, 1, tiled=True)
    attn_rows = jnp.sum(attn_blocks.astype(jnp.float32), axis=1)
    token_rows = lax.dynamic_slice_in_dim(tokens, row_start, row_count, 1)
    normed_rows = layer_norm(
        token_rows.astype(jnp.float32) + attn_rows, norm_gain[0], norm_shift[0]
    ).astype(jnp.bfloat16)
    hidden = jax.nn.gelu(
        jnp.einsum("pld,df->plf", normed_rows, up_weight, preferred_element_type=jnp.float32),
        approximate=False,
    ).astype(jnp.bfloat16)
    hidden = hidden.reshape(prompts, row_count, heads_axis, hidden_block)
    down_blocks = down_weight_t.reshape(model_width, heads_axis, hidden_block)
    mlp_blocks = jnp.einsum(
        "plbf,ebf->plbe", hidden, down_blocks, preferred_element_type=jnp.float32
    ).astype(jnp.bfloat16)
    mlp_rows = jnp.sum(mlp_blocks.astype(jnp.float32), axis=2)
    finished = layer_norm(normed_rows.astype(jnp.float32) + mlp_rows, norm_gain[1], norm_shift[1])
    inside_rows = lax.dynamic_slice_in_dim(inside, row_start, row_count, 1)
    encoded = jnp.where(inside_rows[:, :, None], finished, 0.0).astype(jnp.bfloat16)
    return (encoded, key_cache, value_cache)


def solution(mesh):
    in_specs = (
        P("seq", None, None),
        P("seq"),
        P(("seq", "head"), None, None),
        P(None, ("seq", "head")),
        P(("seq", "head"), None),
        P(None, ("seq", "head")),
        P(),
        P(),
    )
    out_specs = (P("seq", "head", None), P("seq", None, "head"), P("seq", None, "head"))
    return jax.shard_map(shards, mesh=mesh, in_specs=in_specs, out_specs=out_specs, check_vma=False)
```

```python
import math

import jax
import jax.numpy as jnp
from jax import lax
from jax.sharding import PartitionSpec as P

DH = 64


EPSILON = 1e-05


def layer_norm(values, gain, shift):
    center = values - jnp.mean(values, axis=-1, keepdims=True)
    spread = jnp.mean(center * center, axis=-1, keepdims=True)
    return center * lax.rsqrt(spread + EPSILON) * gain + shift


def regroup_weights(attn_in, attn_out, mlp_in, mlp_out, heads_axis, seq_axis):
    rows = attn_in.shape[0]
    model_width = attn_in.shape[2]
    hidden_width = mlp_in.shape[1]
    block_width = model_width // heads_axis
    in_piece = attn_in.astype(jnp.bfloat16).reshape(rows, 3, heads_axis, block_width)
    in_piece = jnp.transpose(in_piece, (0, 2, 1, 3)).reshape(rows, heads_axis, 3 * block_width)
    out_piece = attn_out.astype(jnp.bfloat16).T.reshape(rows, heads_axis, block_width)
    mlp_rows = jnp.concatenate(
        [mlp_in.astype(jnp.bfloat16), mlp_out.astype(jnp.bfloat16).T], axis=1)
    mlp_piece = jnp.broadcast_to(mlp_rows[:, None], (rows, heads_axis, 2 * hidden_width))
    packed = jnp.concatenate([in_piece, out_piece, mlp_piece], axis=2)
    packed = lax.all_to_all(packed, "head", 1, 0, tiled=True)
    packed = packed.reshape(rows * heads_axis, packed.shape[2])
    attn_part = packed[:, :4 * block_width]
    attn_part = jnp.broadcast_to(attn_part[None], (seq_axis,) + attn_part.shape)
    attn_whole = lax.all_to_all(attn_part, "seq", 0, 0, tiled=True)
    attn_whole = attn_whole.reshape(-1, 4 * block_width)
    qkv_weight = attn_whole[:, :3 * block_width].reshape(-1, 3, block_width)
    proj_weight_t = attn_whole[:, 3 * block_width:]
    mlp_whole = lax.all_gather(packed[:, 4 * block_width:], "seq", axis=0, tiled=True)
    return qkv_weight, proj_weight_t, mlp_whole[:, :hidden_width], mlp_whole[:, hidden_width:]


def shards(tokens, lengths, attn_in, attn_out, mlp_in, mlp_out, norm_gain, norm_shift):
    heads_axis = lax.axis_size("head")
    head_index = lax.axis_index("head")
    prompts = tokens.shape[0]
    seq_len = tokens.shape[1]
    model_width = tokens.shape[2]
    hidden_width = mlp_in.shape[1]
    block_width = model_width // heads_axis
    hidden_block = hidden_width // heads_axis
    local_heads = block_width // DH
    qkv_weight, proj_weight_t, up_weight, down_weight_t = regroup_weights(
        attn_in, attn_out, mlp_in, mlp_out, heads_axis, lax.axis_size("seq"))
    projected = jnp.einsum(
        "pld,dte->plte", tokens, qkv_weight, preferred_element_type=jnp.float32
    ).astype(jnp.bfloat16)
    positions = jnp.arange(seq_len, dtype=jnp.int32)
    inside = positions[None, :] < lengths[:, None]
    key_part = projected[:, :, 1]
    value_part = projected[:, :, 2]
    queries = projected[:, :, 0].reshape(prompts, seq_len, local_heads, DH)
    key_heads = key_part.reshape(prompts, seq_len, local_heads, DH)
    value_heads = value_part.reshape(prompts, seq_len, local_heads, DH)
    scores = jnp.einsum(
        "pqhd,pkhd->phqk", queries, key_heads, preferred_element_type=jnp.float32
    ) * (1.0 / math.sqrt(DH))
    scores = jnp.where(inside[:, None, None, :], scores, -1e30)
    row_peak = jnp.max(scores, axis=-1, keepdims=True)
    raised = jnp.exp(scores - row_peak)
    weights = (raised / jnp.sum(raised, axis=-1, keepdims=True)).astype(jnp.bfloat16)
    context = jnp.einsum(
        "phqk,pkhd->pqhd", weights, value_heads, preferred_element_type=jnp.float32
    )
    context = context.astype(jnp.bfloat16).reshape(prompts, seq_len, block_width)
    key_cache = jnp.where(inside[:, :, None], key_part, jnp.zeros_like(key_part))
    value_cache = jnp.where(inside[:, :, None], value_part, jnp.zeros_like(value_part))
    row_count = seq_len // heads_axis
    row_start = head_index * row_count
    attn_partial = jnp.einsum(
        "pld,ed->ple", context, proj_weight_t, preferred_element_type=jnp.float32
    ).astype(jnp.bfloat16)
    attn_blocks = lax.all_to_all(
        attn_partial.reshape(prompts, heads_axis, row_count, model_width), "head", 1, 1, tiled=True)
    attn_rows = jnp.sum(attn_blocks.astype(jnp.float32), axis=1)
    token_rows = lax.dynamic_slice_in_dim(tokens, row_start, row_count, 1)
    normed_rows = layer_norm(
        token_rows.astype(jnp.float32) + attn_rows, norm_gain[0], norm_shift[0]
    ).astype(jnp.bfloat16)
    hidden = jax.nn.gelu(
        jnp.einsum("pld,df->plf", normed_rows, up_weight, preferred_element_type=jnp.float32),
        approximate=False,
    ).astype(jnp.bfloat16)
    hidden = hidden.reshape(prompts, row_count, heads_axis, hidden_block)
    down_blocks = down_weight_t.reshape(model_width, heads_axis, hidden_block)
    mlp_blocks = jnp.einsum(
        "plbf,ebf->plbe", hidden, down_blocks, preferred_element_type=jnp.float32
    ).astype(jnp.bfloat16)
    mlp_rows = jnp.sum(mlp_blocks.astype(jnp.float32), axis=2)
    finished = layer_norm(normed_rows.astype(jnp.float32) + mlp_rows, norm_gain[1], norm_shift[1])
    inside_rows = lax.dynamic_slice_in_dim(inside, row_start, row_count, 1)
    encoded = jnp.where(inside_rows[:, :, None], finished, 0.0).astype(jnp.bfloat16)
    return (encoded, key_cache, value_cache)


def solution(mesh):
    in_specs = (
        P("seq", None, None),
        P("seq"),
        P(("seq", "head"), None, None),
        P(None, ("seq", "head")),
        P(("seq", "head"), None),
        P(None, ("seq", "head")),
        P(),
        P(),
    )
    out_specs = (P("seq", "head", None), P("seq", None, "head"), P("seq", None, "head"))
    return jax.shard_map(shards, mesh=mesh, in_specs=in_specs, out_specs=out_specs, check_vma=False)
```

```python
import math

import jax
import jax.numpy as jnp
from jax import lax
from jax.sharding import PartitionSpec as P

DH = 64


EPSILON = 1e-05
CHUNKS = 4


def layer_norm(values, gain, shift):
    center = values - jnp.mean(values, axis=-1, keepdims=True)
    spread = jnp.mean(center * center, axis=-1, keepdims=True)
    return center * lax.rsqrt(spread + EPSILON) * gain + shift


def regroup_weights(attn_in, attn_out, mlp_in, mlp_out, heads_axis, seq_axis):
    rows = attn_in.shape[0]
    model_width = attn_in.shape[2]
    hidden_width = mlp_in.shape[1]
    block_width = model_width // heads_axis
    in_piece = attn_in.astype(jnp.bfloat16).reshape(rows, 3, heads_axis, block_width)
    in_piece = jnp.transpose(in_piece, (0, 2, 1, 3)).reshape(rows, heads_axis, 3 * block_width)
    out_piece = attn_out.astype(jnp.bfloat16).T.reshape(rows, heads_axis, block_width)
    mlp_rows = jnp.concatenate(
        [mlp_in.astype(jnp.bfloat16), mlp_out.astype(jnp.bfloat16).T], axis=1)
    mlp_piece = jnp.broadcast_to(mlp_rows[:, None], (rows, heads_axis, 2 * hidden_width))
    packed = jnp.concatenate([in_piece, out_piece, mlp_piece], axis=2)
    packed = lax.all_to_all(packed, "head", 1, 0, tiled=True)
    packed = packed.reshape(rows * heads_axis, packed.shape[2])
    attn_part = packed[:, :4 * block_width]
    attn_part = jnp.broadcast_to(attn_part[None], (seq_axis,) + attn_part.shape)
    attn_whole = lax.all_to_all(attn_part, "seq", 0, 0, tiled=True)
    attn_whole = attn_whole.reshape(-1, 4 * block_width)
    qkv_weight = attn_whole[:, :3 * block_width].reshape(-1, 3, block_width)
    proj_weight_t = attn_whole[:, 3 * block_width:]
    up_weight = lax.all_gather(
        packed[:, 4 * block_width:4 * block_width + hidden_width], "seq", axis=0, tiled=True)
    down_weight_t = lax.all_gather(
        packed[:, 4 * block_width + hidden_width:], "seq", axis=0, tiled=True)
    return qkv_weight, proj_weight_t, up_weight, down_weight_t


def encode_chunk(tokens, lengths, qkv_weight, proj_weight_t, up_weight, down_weight_t,
                 norm_gain, norm_shift, heads_axis, head_index):
    prompts = tokens.shape[0]
    seq_len = tokens.shape[1]
    model_width = tokens.shape[2]
    hidden_width = up_weight.shape[1]
    block_width = model_width // heads_axis
    hidden_block = hidden_width // heads_axis
    local_heads = block_width // DH
    row_count = seq_len // heads_axis
    row_start = head_index * row_count
    projected = jnp.einsum(
        "pld,dte->plte", tokens, qkv_weight, preferred_element_type=jnp.float32
    ).astype(jnp.bfloat16)
    positions = jnp.arange(seq_len, dtype=jnp.int32)
    inside = positions[None, :] < lengths[:, None]
    key_part = projected[:, :, 1]
    value_part = projected[:, :, 2]
    queries = projected[:, :, 0].reshape(prompts, seq_len, local_heads, DH)
    key_heads = key_part.reshape(prompts, seq_len, local_heads, DH)
    value_heads = value_part.reshape(prompts, seq_len, local_heads, DH)
    scores = jnp.einsum(
        "pqhd,pkhd->phqk", queries, key_heads, preferred_element_type=jnp.float32
    ) * (1.0 / math.sqrt(DH))
    scores = jnp.where(inside[:, None, None, :], scores, -1e30)
    row_peak = jnp.max(scores, axis=-1, keepdims=True)
    raised = jnp.exp(scores - row_peak)
    weights = (raised / jnp.sum(raised, axis=-1, keepdims=True)).astype(jnp.bfloat16)
    context = jnp.einsum(
        "phqk,pkhd->pqhd", weights, value_heads, preferred_element_type=jnp.float32
    )
    context = context.astype(jnp.bfloat16).reshape(prompts, heads_axis, row_count, block_width)
    key_cache = jnp.where(inside[:, :, None], key_part, jnp.zeros_like(key_part))
    value_cache = jnp.where(inside[:, :, None], value_part, jnp.zeros_like(value_part))
    attn_partial = jnp.einsum(
        "pjrd,ed->jpre", context, proj_weight_t, preferred_element_type=jnp.float32
    ).astype(jnp.bfloat16)
    attn_blocks = lax.all_to_all(attn_partial, "head", 0, 0, tiled=True)
    attn_rows = jnp.sum(attn_blocks.astype(jnp.float32), axis=0)
    token_rows = lax.dynamic_slice_in_dim(tokens, row_start, row_count, 1)
    normed_rows = layer_norm(
        token_rows.astype(jnp.float32) + attn_rows, norm_gain[0], norm_shift[0]
    ).astype(jnp.bfloat16)
    hidden = jax.nn.gelu(
        jnp.einsum("pld,df->plf", normed_rows, up_weight, preferred_element_type=jnp.float32),
        approximate=False,
    ).astype(jnp.bfloat16)
    hidden = hidden.reshape(prompts, row_count, heads_axis, hidden_block)
    down_blocks = down_weight_t.reshape(model_width, heads_axis, hidden_block)
    mlp_blocks = jnp.einsum(
        "plbf,ebf->plbe", hidden, down_blocks, preferred_element_type=jnp.float32
    ).astype(jnp.bfloat16)
    mlp_rows = jnp.sum(mlp_blocks.astype(jnp.float32), axis=2)
    finished = layer_norm(normed_rows.astype(jnp.float32) + mlp_rows, norm_gain[1], norm_shift[1])
    inside_rows = lax.dynamic_slice_in_dim(inside, row_start, row_count, 1)
    encoded = jnp.where(inside_rows[:, :, None], finished, 0.0).astype(jnp.bfloat16)
    return encoded, key_cache, value_cache


def shards(tokens, lengths, attn_in, attn_out, mlp_in, mlp_out, norm_gain, norm_shift):
    heads_axis = lax.axis_size("head")
    head_index = lax.axis_index("head")
    qkv_weight, proj_weight_t, up_weight, down_weight_t = regroup_weights(
        attn_in, attn_out, mlp_in, mlp_out, heads_axis, lax.axis_size("seq"))
    prompts = tokens.shape[0]
    chunk = max(1, prompts // CHUNKS)
    pieces = []
    for lower in range(0, prompts, chunk):
        pieces.append(encode_chunk(
            tokens[lower:lower + chunk], lengths[lower:lower + chunk], qkv_weight,
            proj_weight_t, up_weight, down_weight_t, norm_gain, norm_shift,
            heads_axis, head_index))
    return tuple(jnp.concatenate(parts, axis=0) for parts in zip(*pieces))


def solution(mesh):
    in_specs = (
        P("seq", None, None),
        P("seq"),
        P(("seq", "head"), None, None),
        P(None, ("seq", "head")),
        P(("seq", "head"), None),
        P(None, ("seq", "head")),
        P(),
        P(),
    )
    out_specs = (P("seq", "head", None), P("seq", None, "head"), P("seq", None, "head"))
    return jax.shard_map(shards, mesh=mesh, in_specs=in_specs, out_specs=out_specs, check_vma=False)
```

```python
import math

import jax
import jax.numpy as jnp
from jax import lax
from jax.sharding import PartitionSpec as P

DH = 64


EPSILON = 1e-05
CHUNKS = 1


def layer_norm(values, gain, shift):
    center = values - jnp.mean(values, axis=-1, keepdims=True)
    spread = jnp.mean(center * center, axis=-1, keepdims=True)
    return center * lax.rsqrt(spread + EPSILON) * gain + shift


def regroup_weights(attn_in, attn_out, mlp_in, mlp_out, heads_axis, seq_axis):
    rows = attn_in.shape[0]
    model_width = attn_in.shape[2]
    hidden_width = mlp_in.shape[1]
    block_width = model_width // heads_axis
    in_piece = attn_in.astype(jnp.bfloat16).reshape(rows, 3, heads_axis, block_width)
    in_piece = jnp.transpose(in_piece, (0, 2, 1, 3)).reshape(rows, heads_axis, 3 * block_width)
    out_piece = attn_out.astype(jnp.bfloat16).T.reshape(rows, heads_axis, block_width)
    mlp_rows = jnp.concatenate(
        [mlp_in.astype(jnp.bfloat16), mlp_out.astype(jnp.bfloat16).T], axis=1)
    mlp_piece = jnp.broadcast_to(mlp_rows[:, None], (rows, heads_axis, 2 * hidden_width))
    packed = jnp.concatenate([in_piece, out_piece, mlp_piece], axis=2)
    packed = lax.all_to_all(packed, "head", 1, 0, tiled=True)
    packed = packed.reshape(rows * heads_axis, packed.shape[2])
    attn_part = packed[:, :4 * block_width]
    attn_part = jnp.broadcast_to(attn_part[None], (seq_axis,) + attn_part.shape)
    attn_whole = lax.all_to_all(attn_part, "seq", 0, 0, tiled=True)
    attn_whole = attn_whole.reshape(-1, 4 * block_width)
    qkv_weight = attn_whole[:, :3 * block_width].reshape(-1, 3, block_width)
    proj_weight_t = attn_whole[:, 3 * block_width:]
    up_weight = lax.all_gather(
        packed[:, 4 * block_width:4 * block_width + hidden_width], "seq", axis=0, tiled=True)
    down_weight_t = lax.all_gather(
        packed[:, 4 * block_width + hidden_width:], "seq", axis=0, tiled=True)
    return qkv_weight, proj_weight_t, up_weight, down_weight_t


def encode_chunk(tokens, lengths, qkv_weight, proj_weight_t, up_weight, down_weight_t,
                 norm_gain, norm_shift, heads_axis, head_index):
    prompts = tokens.shape[0]
    seq_len = tokens.shape[1]
    model_width = tokens.shape[2]
    hidden_width = up_weight.shape[1]
    block_width = model_width // heads_axis
    hidden_block = hidden_width // heads_axis
    local_heads = block_width // DH
    row_count = seq_len // heads_axis
    row_start = head_index * row_count
    projected = jnp.einsum(
        "pld,dte->plte", tokens, qkv_weight, preferred_element_type=jnp.float32
    ).astype(jnp.bfloat16)
    positions = jnp.arange(seq_len, dtype=jnp.int32)
    inside = positions[None, :] < lengths[:, None]
    key_part = projected[:, :, 1]
    value_part = projected[:, :, 2]
    queries = projected[:, :, 0].reshape(prompts, seq_len, local_heads, DH)
    key_heads = key_part.reshape(prompts, seq_len, local_heads, DH)
    value_heads = value_part.reshape(prompts, seq_len, local_heads, DH)
    scores = jnp.einsum(
        "pqhd,pkhd->phqk", queries, key_heads, preferred_element_type=jnp.float32
    ) * (1.0 / math.sqrt(DH))
    scores = jnp.where(inside[:, None, None, :], scores, -1e30)
    row_peak = jnp.max(scores, axis=-1, keepdims=True)
    raised = jnp.exp(scores - row_peak)
    weights = (raised / jnp.sum(raised, axis=-1, keepdims=True)).astype(jnp.bfloat16)
    context = jnp.einsum(
        "phqk,pkhd->pqhd", weights, value_heads, preferred_element_type=jnp.float32
    )
    context = context.astype(jnp.bfloat16).reshape(prompts, heads_axis, row_count, block_width)
    key_cache = jnp.where(inside[:, :, None], key_part, jnp.zeros_like(key_part))
    value_cache = jnp.where(inside[:, :, None], value_part, jnp.zeros_like(value_part))
    attn_partial = jnp.einsum(
        "pjrd,ed->jpre", context, proj_weight_t, preferred_element_type=jnp.float32
    ).astype(jnp.bfloat16)
    attn_blocks = lax.all_to_all(attn_partial, "head", 0, 0, tiled=True)
    attn_rows = jnp.sum(attn_blocks.astype(jnp.float32), axis=0)
    token_rows = lax.dynamic_slice_in_dim(tokens, row_start, row_count, 1)
    normed_rows = layer_norm(
        token_rows.astype(jnp.float32) + attn_rows, norm_gain[0], norm_shift[0]
    ).astype(jnp.bfloat16)
    hidden = jax.nn.gelu(
        jnp.einsum("pld,df->plf", normed_rows, up_weight, preferred_element_type=jnp.float32),
        approximate=False,
    ).astype(jnp.bfloat16)
    hidden = hidden.reshape(prompts, row_count, heads_axis, hidden_block)
    down_blocks = down_weight_t.reshape(model_width, heads_axis, hidden_block)
    mlp_blocks = jnp.einsum(
        "plbf,ebf->plbe", hidden, down_blocks, preferred_element_type=jnp.float32
    ).astype(jnp.bfloat16)
    mlp_rows = jnp.sum(mlp_blocks.astype(jnp.float32), axis=2)
    finished = layer_norm(normed_rows.astype(jnp.float32) + mlp_rows, norm_gain[1], norm_shift[1])
    inside_rows = lax.dynamic_slice_in_dim(inside, row_start, row_count, 1)
    encoded = jnp.where(inside_rows[:, :, None], finished, 0.0).astype(jnp.bfloat16)
    return encoded, key_cache, value_cache


def shards(tokens, lengths, attn_in, attn_out, mlp_in, mlp_out, norm_gain, norm_shift):
    heads_axis = lax.axis_size("head")
    head_index = lax.axis_index("head")
    qkv_weight, proj_weight_t, up_weight, down_weight_t = regroup_weights(
        attn_in, attn_out, mlp_in, mlp_out, heads_axis, lax.axis_size("seq"))
    prompts = tokens.shape[0]
    chunk = max(1, prompts // CHUNKS)
    pieces = []
    for lower in range(0, prompts, chunk):
        pieces.append(encode_chunk(
            tokens[lower:lower + chunk], lengths[lower:lower + chunk], qkv_weight,
            proj_weight_t, up_weight, down_weight_t, norm_gain, norm_shift,
            heads_axis, head_index))
    return tuple(jnp.concatenate(parts, axis=0) for parts in zip(*pieces))


def solution(mesh):
    in_specs = (
        P("seq", None, None),
        P("seq"),
        P(("seq", "head"), None, None),
        P(None, ("seq", "head")),
        P(("seq", "head"), None),
        P(None, ("seq", "head")),
        P(),
        P(),
    )
    out_specs = (P("seq", "head", None), P("seq", None, "head"), P("seq", None, "head"))
    return jax.shard_map(shards, mesh=mesh, in_specs=in_specs, out_specs=out_specs, check_vma=False)
```

```python
import math

import jax
import jax.numpy as jnp
from jax import lax
from jax.sharding import PartitionSpec as P

DH = 64


EPSILON = 1e-05
CHUNKS = 1


def layer_norm(values, gain, shift):
    center = values - jnp.mean(values, axis=-1, keepdims=True)
    spread = jnp.mean(center * center, axis=-1, keepdims=True)
    return center * lax.rsqrt(spread + EPSILON) * gain + shift


def regroup_weights(attn_in, attn_out, mlp_in, mlp_out, heads_axis, seq_axis):
    rows = attn_in.shape[0]
    model_width = attn_in.shape[2]
    hidden_width = mlp_in.shape[1]
    block_width = model_width // heads_axis
    in_piece = attn_in.astype(jnp.bfloat16).reshape(rows, 3, heads_axis, block_width)
    in_piece = jnp.transpose(in_piece, (0, 2, 1, 3)).reshape(rows, heads_axis, 3 * block_width)
    whole_rows = jnp.concatenate(
        [attn_out.astype(jnp.bfloat16).T, mlp_in.astype(jnp.bfloat16),
         mlp_out.astype(jnp.bfloat16).T], axis=1)
    whole_piece = jnp.broadcast_to(whole_rows[:, None], (rows, heads_axis, whole_rows.shape[1]))
    packed = jnp.concatenate([in_piece, whole_piece], axis=2)
    packed = lax.all_to_all(packed, "head", 1, 0, tiled=True)
    packed = packed.reshape(rows * heads_axis, packed.shape[2])
    in_part = packed[:, :3 * block_width]
    in_part = jnp.broadcast_to(in_part[None], (seq_axis,) + in_part.shape)
    qkv_weight = lax.all_to_all(in_part, "seq", 0, 0, tiled=True)
    qkv_weight = qkv_weight.reshape(-1, 3, block_width)
    edges = [3 * block_width, 3 * block_width + model_width,
             3 * block_width + model_width + hidden_width,
             3 * block_width + model_width + 2 * hidden_width]
    proj_weight_t, up_weight, down_weight_t = [
        lax.all_gather(packed[:, lower:upper], "seq", axis=0, tiled=True)
        for lower, upper in zip(edges[:-1], edges[1:])]
    return qkv_weight, proj_weight_t, up_weight, down_weight_t


def encode_chunk(tokens, lengths, qkv_weight, proj_weight_t, up_weight, down_weight_t,
                 norm_gain, norm_shift, heads_axis, head_index):
    prompts = tokens.shape[0]
    seq_len = tokens.shape[1]
    model_width = tokens.shape[2]
    hidden_width = up_weight.shape[1]
    block_width = model_width // heads_axis
    hidden_block = hidden_width // heads_axis
    local_heads = block_width // DH
    row_count = seq_len // heads_axis
    row_start = head_index * row_count
    projected = jnp.einsum(
        "pld,dte->plte", tokens, qkv_weight, preferred_element_type=jnp.float32
    ).astype(jnp.bfloat16)
    positions = jnp.arange(seq_len, dtype=jnp.int32)
    inside = positions[None, :] < lengths[:, None]
    key_part = projected[:, :, 1]
    value_part = projected[:, :, 2]
    queries = projected[:, :, 0].reshape(prompts, seq_len, local_heads, DH)
    key_heads = key_part.reshape(prompts, seq_len, local_heads, DH)
    value_heads = value_part.reshape(prompts, seq_len, local_heads, DH)
    scores = jnp.einsum(
        "pqhd,pkhd->phqk", queries, key_heads, preferred_element_type=jnp.float32
    ) * (1.0 / math.sqrt(DH))
    scores = jnp.where(inside[:, None, None, :], scores, -1e30)
    row_peak = jnp.max(scores, axis=-1, keepdims=True)
    raised = jnp.exp(scores - row_peak)
    weights = (raised / jnp.sum(raised, axis=-1, keepdims=True)).astype(jnp.bfloat16)
    context = jnp.einsum(
        "phqk,pkhd->pqhd", weights, value_heads, preferred_element_type=jnp.float32
    )
    context = context.astype(jnp.bfloat16).reshape(prompts, heads_axis, row_count, block_width)
    key_cache = jnp.where(inside[:, :, None], key_part, jnp.zeros_like(key_part))
    value_cache = jnp.where(inside[:, :, None], value_part, jnp.zeros_like(value_part))
    context_blocks = jnp.transpose(context, (1, 0, 2, 3))
    context_blocks = lax.all_to_all(context_blocks, "head", 0, 0, tiled=True)
    proj_blocks = proj_weight_t.reshape(model_width, heads_axis, block_width)
    attn_blocks = jnp.einsum(
        "sprf,esf->spre", context_blocks, proj_blocks, preferred_element_type=jnp.float32
    ).astype(jnp.bfloat16)
    attn_rows = jnp.sum(attn_blocks.astype(jnp.float32), axis=0)
    token_rows = lax.dynamic_slice_in_dim(tokens, row_start, row_count, 1)
    normed_rows = layer_norm(
        token_rows.astype(jnp.float32) + attn_rows, norm_gain[0], norm_shift[0]
    ).astype(jnp.bfloat16)
    hidden = jax.nn.gelu(
        jnp.einsum("pld,df->plf", normed_rows, up_weight, preferred_element_type=jnp.float32),
        approximate=False,
    ).astype(jnp.bfloat16)
    hidden = hidden.reshape(prompts, row_count, heads_axis, hidden_block)
    down_blocks = down_weight_t.reshape(model_width, heads_axis, hidden_block)
    mlp_blocks = jnp.einsum(
        "plbf,ebf->plbe", hidden, down_blocks, preferred_element_type=jnp.float32
    ).astype(jnp.bfloat16)
    mlp_rows = jnp.sum(mlp_blocks.astype(jnp.float32), axis=2)
    finished = layer_norm(normed_rows.astype(jnp.float32) + mlp_rows, norm_gain[1], norm_shift[1])
    inside_rows = lax.dynamic_slice_in_dim(inside, row_start, row_count, 1)
    encoded = jnp.where(inside_rows[:, :, None], finished, 0.0).astype(jnp.bfloat16)
    return encoded, key_cache, value_cache


def shards(tokens, lengths, attn_in, attn_out, mlp_in, mlp_out, norm_gain, norm_shift):
    heads_axis = lax.axis_size("head")
    head_index = lax.axis_index("head")
    qkv_weight, proj_weight_t, up_weight, down_weight_t = regroup_weights(
        attn_in, attn_out, mlp_in, mlp_out, heads_axis, lax.axis_size("seq"))
    prompts = tokens.shape[0]
    chunk = max(1, prompts // CHUNKS)
    pieces = []
    for lower in range(0, prompts, chunk):
        pieces.append(encode_chunk(
            tokens[lower:lower + chunk], lengths[lower:lower + chunk], qkv_weight,
            proj_weight_t, up_weight, down_weight_t, norm_gain, norm_shift,
            heads_axis, head_index))
    return tuple(jnp.concatenate(parts, axis=0) for parts in zip(*pieces))


def solution(mesh):
    in_specs = (
        P("seq", None, None),
        P("seq"),
        P(("seq", "head"), None, None),
        P(None, ("seq", "head")),
        P(("seq", "head"), None),
        P(None, ("seq", "head")),
        P(),
        P(),
    )
    out_specs = (P("seq", "head", None), P("seq", None, "head"), P("seq", None, "head"))
    return jax.shard_map(shards, mesh=mesh, in_specs=in_specs, out_specs=out_specs, check_vma=False)
```

```python
import math

import jax
import jax.numpy as jnp
from jax import lax
from jax.sharding import PartitionSpec as P

DH = 64


EPSILON = 1e-05
CHUNKS = 1


def layer_norm(values, gain, shift):
    center = values - jnp.mean(values, axis=-1, keepdims=True)
    spread = jnp.mean(center * center, axis=-1, keepdims=True)
    return center * lax.rsqrt(spread + EPSILON) * gain + shift


def regroup_weights(attn_in, attn_out, mlp_in, mlp_out, heads_axis, seq_axis):
    rows = attn_in.shape[0]
    model_width = attn_in.shape[2]
    hidden_width = mlp_in.shape[1]
    block_width = model_width // heads_axis
    in_piece = attn_in.astype(jnp.bfloat16).reshape(rows, 3, heads_axis, block_width)
    in_piece = jnp.transpose(in_piece, (0, 2, 1, 3)).reshape(rows, heads_axis, 3 * block_width)
    whole_rows = jnp.concatenate(
        [attn_out.astype(jnp.bfloat16).T, mlp_in.astype(jnp.bfloat16),
         mlp_out.astype(jnp.bfloat16).T], axis=1)
    whole_piece = jnp.broadcast_to(whole_rows[:, None], (rows, heads_axis, whole_rows.shape[1]))
    packed = jnp.concatenate([in_piece, whole_piece], axis=2)
    packed = lax.all_to_all(packed, "head", 1, 0, tiled=True)
    packed = packed.reshape(rows * heads_axis, packed.shape[2])
    attn_width = 3 * block_width + model_width
    attn_part = packed[:, :attn_width]
    attn_part = jnp.broadcast_to(attn_part[None], (seq_axis,) + attn_part.shape)
    attn_whole = lax.all_to_all(attn_part, "seq", 0, 0, tiled=True)
    attn_whole = attn_whole.reshape(-1, attn_width)
    qkv_weight = attn_whole[:, :3 * block_width].reshape(-1, 3, block_width)
    proj_weight_t = attn_whole[:, 3 * block_width:]
    up_weight, down_weight_t = [
        lax.all_gather(packed[:, lower:lower + hidden_width], "seq", axis=0, tiled=True)
        for lower in (attn_width, attn_width + hidden_width)]
    return qkv_weight, proj_weight_t, up_weight, down_weight_t


def encode_chunk(tokens, lengths, qkv_weight, proj_weight_t, up_weight, down_weight_t,
                 norm_gain, norm_shift, heads_axis, head_index):
    prompts = tokens.shape[0]
    seq_len = tokens.shape[1]
    model_width = tokens.shape[2]
    hidden_width = up_weight.shape[1]
    block_width = model_width // heads_axis
    hidden_block = hidden_width // heads_axis
    local_heads = block_width // DH
    row_count = seq_len // heads_axis
    row_start = head_index * row_count
    projected = jnp.einsum(
        "pld,dte->plte", tokens, qkv_weight, preferred_element_type=jnp.float32
    ).astype(jnp.bfloat16)
    positions = jnp.arange(seq_len, dtype=jnp.int32)
    inside = positions[None, :] < lengths[:, None]
    key_part = projected[:, :, 1]
    value_part = projected[:, :, 2]
    queries = projected[:, :, 0].reshape(prompts, seq_len, local_heads, DH)
    key_heads = key_part.reshape(prompts, seq_len, local_heads, DH)
    value_heads = value_part.reshape(prompts, seq_len, local_heads, DH)
    scores = jnp.einsum(
        "pqhd,pkhd->phqk", queries, key_heads, preferred_element_type=jnp.float32
    ) * (1.0 / math.sqrt(DH))
    scores = jnp.where(inside[:, None, None, :], scores, -1e30)
    row_peak = jnp.max(scores, axis=-1, keepdims=True)
    raised = jnp.exp(scores - row_peak)
    weights = (raised / jnp.sum(raised, axis=-1, keepdims=True)).astype(jnp.bfloat16)
    context = jnp.einsum(
        "phqk,pkhd->pqhd", weights, value_heads, preferred_element_type=jnp.float32
    )
    context = context.astype(jnp.bfloat16).reshape(prompts, heads_axis, row_count, block_width)
    key_cache = jnp.where(inside[:, :, None], key_part, jnp.zeros_like(key_part))
    value_cache = jnp.where(inside[:, :, None], value_part, jnp.zeros_like(value_part))
    context_blocks = jnp.transpose(context, (1, 0, 2, 3))
    context_blocks = lax.all_to_all(context_blocks, "head", 0, 0, tiled=True)
    proj_blocks = proj_weight_t.reshape(model_width, heads_axis, block_width)
    attn_blocks = jnp.einsum(
        "sprf,esf->spre", context_blocks, proj_blocks, preferred_element_type=jnp.float32
    ).astype(jnp.bfloat16)
    attn_rows = jnp.sum(attn_blocks.astype(jnp.float32), axis=0)
    token_rows = lax.dynamic_slice_in_dim(tokens, row_start, row_count, 1)
    normed_rows = layer_norm(
        token_rows.astype(jnp.float32) + attn_rows, norm_gain[0], norm_shift[0]
    ).astype(jnp.bfloat16)
    hidden = jax.nn.gelu(
        jnp.einsum("pld,df->plf", normed_rows, up_weight, preferred_element_type=jnp.float32),
        approximate=False,
    ).astype(jnp.bfloat16)
    hidden = hidden.reshape(prompts, row_count, heads_axis, hidden_block)
    down_blocks = down_weight_t.reshape(model_width, heads_axis, hidden_block)
    mlp_blocks = jnp.einsum(
        "plbf,ebf->plbe", hidden, down_blocks, preferred_element_type=jnp.float32
    ).astype(jnp.bfloat16)
    mlp_rows = jnp.sum(mlp_blocks.astype(jnp.float32), axis=2)
    finished = layer_norm(normed_rows.astype(jnp.float32) + mlp_rows, norm_gain[1], norm_shift[1])
    inside_rows = lax.dynamic_slice_in_dim(inside, row_start, row_count, 1)
    encoded = jnp.where(inside_rows[:, :, None], finished, 0.0).astype(jnp.bfloat16)
    return encoded, key_cache, value_cache


def shards(tokens, lengths, attn_in, attn_out, mlp_in, mlp_out, norm_gain, norm_shift):
    heads_axis = lax.axis_size("head")
    head_index = lax.axis_index("head")
    qkv_weight, proj_weight_t, up_weight, down_weight_t = regroup_weights(
        attn_in, attn_out, mlp_in, mlp_out, heads_axis, lax.axis_size("seq"))
    prompts = tokens.shape[0]
    chunk = max(1, prompts // CHUNKS)
    pieces = []
    for lower in range(0, prompts, chunk):
        pieces.append(encode_chunk(
            tokens[lower:lower + chunk], lengths[lower:lower + chunk], qkv_weight,
            proj_weight_t, up_weight, down_weight_t, norm_gain, norm_shift,
            heads_axis, head_index))
    return tuple(jnp.concatenate(parts, axis=0) for parts in zip(*pieces))


def solution(mesh):
    in_specs = (
        P("seq", None, None),
        P("seq"),
        P(("seq", "head"), None, None),
        P(None, ("seq", "head")),
        P(("seq", "head"), None),
        P(None, ("seq", "head")),
        P(),
        P(),
    )
    out_specs = (P("seq", "head", None), P("seq", None, "head"), P("seq", None, "head"))
    return jax.shard_map(shards, mesh=mesh, in_specs=in_specs, out_specs=out_specs, check_vma=False)
```

```python
import math

import jax
import jax.numpy as jnp
from jax import lax
from jax.sharding import PartitionSpec as P

DH = 64


EPSILON = 1e-05
CHUNKS = 1


def layer_norm(values, gain, shift):
    center = values - jnp.mean(values, axis=-1, keepdims=True)
    spread = jnp.mean(center * center, axis=-1, keepdims=True)
    return center * lax.rsqrt(spread + EPSILON) * gain + shift


def regroup_weights(attn_in, attn_out, mlp_in, mlp_out, heads_axis, seq_axis):
    rows = attn_in.shape[0]
    model_width = attn_in.shape[2]
    hidden_width = mlp_in.shape[1]
    block_width = model_width // heads_axis
    in_piece = attn_in.astype(jnp.bfloat16).reshape(rows, 3, heads_axis, block_width)
    in_piece = jnp.transpose(in_piece, (0, 2, 1, 3)).reshape(rows, heads_axis, 3 * block_width)
    down_rows = mlp_out.astype(jnp.bfloat16).T
    half = hidden_width // 2
    whole_rows = jnp.concatenate(
        [attn_out.astype(jnp.bfloat16).T, mlp_in.astype(jnp.bfloat16), down_rows[:, :half]], axis=1)
    whole_piece = jnp.broadcast_to(whole_rows[:, None], (rows, heads_axis, whole_rows.shape[1]))
    packed = jnp.concatenate([in_piece, whole_piece], axis=2)
    packed = lax.all_to_all(packed, "head", 1, 0, tiled=True)
    packed = packed.reshape(rows * heads_axis, packed.shape[2])
    in_part = packed[:, :3 * block_width]
    in_part = jnp.broadcast_to(in_part[None], (seq_axis,) + in_part.shape)
    qkv_weight = lax.all_to_all(in_part, "seq", 0, 0, tiled=True)
    qkv_weight = qkv_weight.reshape(-1, 3, block_width)
    edges = [3 * block_width, 3 * block_width + model_width,
             3 * block_width + model_width + hidden_width,
             3 * block_width + model_width + hidden_width + half]
    proj_weight_t, up_weight = [
        lax.all_gather(packed[:, lower:upper], "seq", axis=0, tiled=True)
        for lower, upper in zip(edges[:-2], edges[1:-1])]
    low_rows, up_weight = lax.optimization_barrier((packed[:, edges[2]:edges[3]], up_weight))
    down_low = lax.all_gather(low_rows, "seq", axis=0, tiled=True)
    down_high = lax.all_gather(down_rows[:, half:], "seq", axis=0, tiled=True)
    return qkv_weight, proj_weight_t, up_weight, (down_low, down_high)


def spread_down(down_low, down_high, heads_axis):
    rows = down_high.shape[0]
    down_high = jnp.broadcast_to(down_high[None], (heads_axis,) + down_high.shape)
    down_high = lax.all_to_all(down_high, "head", 0, 0, tiled=True)
    seq_axis = lax.axis_size("seq")
    down_high = down_high.reshape(heads_axis, seq_axis, rows // seq_axis, -1)
    down_high = jnp.transpose(down_high, (1, 0, 2, 3)).reshape(heads_axis * rows, -1)
    return jnp.concatenate([down_low, down_high], axis=1)


def encode_chunk(tokens, lengths, qkv_weight, proj_weight_t, up_weight, down_weight_t,
                 norm_gain, norm_shift, heads_axis, head_index):
    prompts = tokens.shape[0]
    seq_len = tokens.shape[1]
    model_width = tokens.shape[2]
    hidden_width = up_weight.shape[1]
    block_width = model_width // heads_axis
    hidden_block = hidden_width // heads_axis
    local_heads = block_width // DH
    row_count = seq_len // heads_axis
    row_start = head_index * row_count
    projected = jnp.einsum(
        "pld,dte->plte", tokens, qkv_weight, preferred_element_type=jnp.float32
    ).astype(jnp.bfloat16)
    down_high, projected = lax.optimization_barrier((down_weight_t[1], projected))
    down_weight_t = spread_down(down_weight_t[0], down_high, heads_axis)
    positions = jnp.arange(seq_len, dtype=jnp.int32)
    inside = positions[None, :] < lengths[:, None]
    key_part = projected[:, :, 1]
    value_part = projected[:, :, 2]
    queries = projected[:, :, 0].reshape(prompts, seq_len, local_heads, DH)
    key_heads = key_part.reshape(prompts, seq_len, local_heads, DH)
    value_heads = value_part.reshape(prompts, seq_len, local_heads, DH)
    scores = jnp.einsum(
        "pqhd,pkhd->phqk", queries, key_heads, preferred_element_type=jnp.float32
    ) * (1.0 / math.sqrt(DH))
    scores = jnp.where(inside[:, None, None, :], scores, -1e30)
    row_peak = jnp.max(scores, axis=-1, keepdims=True)
    raised = jnp.exp(scores - row_peak)
    weights = (raised / jnp.sum(raised, axis=-1, keepdims=True)).astype(jnp.bfloat16)
    context = jnp.einsum(
        "phqk,pkhd->pqhd", weights, value_heads, preferred_element_type=jnp.float32
    )
    context = context.astype(jnp.bfloat16).reshape(prompts, heads_axis, row_count, block_width)
    key_cache = jnp.where(inside[:, :, None], key_part, jnp.zeros_like(key_part))
    value_cache = jnp.where(inside[:, :, None], value_part, jnp.zeros_like(value_part))
    context_blocks = jnp.transpose(context, (1, 0, 2, 3))
    context_blocks = lax.all_to_all(context_blocks, "head", 0, 0, tiled=True)
    proj_blocks = proj_weight_t.reshape(model_width, heads_axis, block_width)
    attn_blocks = jnp.einsum(
        "sprf,esf->spre", context_blocks, proj_blocks, preferred_element_type=jnp.float32
    ).astype(jnp.bfloat16)
    attn_rows = jnp.sum(attn_blocks.astype(jnp.float32), axis=0)
    token_rows = lax.dynamic_slice_in_dim(tokens, row_start, row_count, 1)
    normed_rows = layer_norm(
        token_rows.astype(jnp.float32) + attn_rows, norm_gain[0], norm_shift[0]
    ).astype(jnp.bfloat16)
    hidden = jax.nn.gelu(
        jnp.einsum("pld,df->plf", normed_rows, up_weight, preferred_element_type=jnp.float32),
        approximate=False,
    ).astype(jnp.bfloat16)
    hidden = hidden.reshape(prompts, row_count, heads_axis, hidden_block)
    down_blocks = down_weight_t.reshape(model_width, heads_axis, hidden_block)
    mlp_blocks = jnp.einsum(
        "plbf,ebf->plbe", hidden, down_blocks, preferred_element_type=jnp.float32
    ).astype(jnp.bfloat16)
    mlp_rows = jnp.sum(mlp_blocks.astype(jnp.float32), axis=2)
    finished = layer_norm(normed_rows.astype(jnp.float32) + mlp_rows, norm_gain[1], norm_shift[1])
    inside_rows = lax.dynamic_slice_in_dim(inside, row_start, row_count, 1)
    encoded = jnp.where(inside_rows[:, :, None], finished, 0.0).astype(jnp.bfloat16)
    return encoded, key_cache, value_cache


def shards(tokens, lengths, attn_in, attn_out, mlp_in, mlp_out, norm_gain, norm_shift):
    heads_axis = lax.axis_size("head")
    head_index = lax.axis_index("head")
    qkv_weight, proj_weight_t, up_weight, down_weight_t = regroup_weights(
        attn_in, attn_out, mlp_in, mlp_out, heads_axis, lax.axis_size("seq"))
    prompts = tokens.shape[0]
    chunk = max(1, prompts // CHUNKS)
    pieces = []
    for lower in range(0, prompts, chunk):
        pieces.append(encode_chunk(
            tokens[lower:lower + chunk], lengths[lower:lower + chunk], qkv_weight,
            proj_weight_t, up_weight, down_weight_t, norm_gain, norm_shift,
            heads_axis, head_index))
    return tuple(jnp.concatenate(parts, axis=0) for parts in zip(*pieces))


def solution(mesh):
    in_specs = (
        P("seq", None, None),
        P("seq"),
        P(("seq", "head"), None, None),
        P(None, ("seq", "head")),
        P(("seq", "head"), None),
        P(None, ("seq", "head")),
        P(),
        P(),
    )
    out_specs = (P("seq", "head", None), P("seq", None, "head"), P("seq", None, "head"))
    return jax.shard_map(shards, mesh=mesh, in_specs=in_specs, out_specs=out_specs, check_vma=False)
```

```python
import math

import jax
import jax.numpy as jnp
from jax import lax
from jax.sharding import PartitionSpec as P

DH = 64


EPSILON = 1e-05
CHUNKS = 1


def layer_norm(values, gain, shift):
    center = values - jnp.mean(values, axis=-1, keepdims=True)
    spread = jnp.mean(center * center, axis=-1, keepdims=True)
    return center * lax.rsqrt(spread + EPSILON) * gain + shift


def regroup_weights(attn_in, attn_out, mlp_in, mlp_out, heads_axis, seq_axis):
    rows = attn_in.shape[0]
    model_width = attn_in.shape[2]
    hidden_width = mlp_in.shape[1]
    block_width = model_width // heads_axis
    up_chunks = hidden_width // model_width
    early = jnp.concatenate(
        [attn_out.astype(jnp.bfloat16).T[None],
         mlp_in.astype(jnp.bfloat16).reshape(rows, up_chunks, model_width).transpose(1, 0, 2)],
        axis=0)
    early = jnp.broadcast_to(early[:, :, None], early.shape[:2] + (heads_axis, model_width))
    early = lax.all_to_all(early, "head", 2, 1, tiled=True)
    early = early.reshape(1 + up_chunks, rows * heads_axis, model_width)
    early = lax.all_gather(early, "seq", axis=1, tiled=True)
    proj_weight_t = early[0]
    up_weight = early[1:]
    in_piece = attn_in.astype(jnp.bfloat16).reshape(rows, 3, heads_axis, block_width)
    in_piece = jnp.transpose(in_piece, (0, 2, 1, 3)).reshape(rows, heads_axis, 3 * block_width)
    down_rows = mlp_out.astype(jnp.bfloat16).T
    down_piece = jnp.broadcast_to(down_rows[:, None], (rows, heads_axis, hidden_width))
    packed = jnp.concatenate([in_piece, down_piece], axis=2)
    packed = lax.all_to_all(packed, "head", 1, 0, tiled=True)
    packed = packed.reshape(rows * heads_axis, packed.shape[2])
    in_part = packed[:, :3 * block_width]
    in_part = jnp.broadcast_to(in_part[None], (seq_axis,) + in_part.shape)
    qkv_weight = lax.all_to_all(in_part, "seq", 0, 0, tiled=True)
    qkv_weight = qkv_weight.reshape(-1, 3, block_width)
    down_weight_t = lax.all_gather(packed[:, 3 * block_width:], "seq", axis=0, tiled=True)
    return qkv_weight, proj_weight_t, up_weight, down_weight_t


def encode_chunk(tokens, lengths, qkv_weight, proj_weight_t, up_weight, down_weight_t,
                 norm_gain, norm_shift, heads_axis, head_index):
    prompts = tokens.shape[0]
    seq_len = tokens.shape[1]
    model_width = tokens.shape[2]
    hidden_width = up_weight.shape[0] * up_weight.shape[2]
    block_width = model_width // heads_axis
    hidden_block = hidden_width // heads_axis
    local_heads = block_width // DH
    row_count = seq_len // heads_axis
    row_start = head_index * row_count
    projected = jnp.einsum(
        "pld,dte->plte", tokens, qkv_weight, preferred_element_type=jnp.float32
    ).astype(jnp.bfloat16)
    positions = jnp.arange(seq_len, dtype=jnp.int32)
    inside = positions[None, :] < lengths[:, None]
    key_part = projected[:, :, 1]
    value_part = projected[:, :, 2]
    queries = projected[:, :, 0].reshape(prompts, seq_len, local_heads, DH)
    key_heads = key_part.reshape(prompts, seq_len, local_heads, DH)
    value_heads = value_part.reshape(prompts, seq_len, local_heads, DH)
    scores = jnp.einsum(
        "pqhd,pkhd->phqk", queries, key_heads, preferred_element_type=jnp.float32
    ) * (1.0 / math.sqrt(DH))
    scores = jnp.where(inside[:, None, None, :], scores, -1e30)
    row_peak = jnp.max(scores, axis=-1, keepdims=True)
    raised = jnp.exp(scores - row_peak)
    weights = (raised / jnp.sum(raised, axis=-1, keepdims=True)).astype(jnp.bfloat16)
    context = jnp.einsum(
        "phqk,pkhd->pqhd", weights, value_heads, preferred_element_type=jnp.float32
    )
    context = context.astype(jnp.bfloat16).reshape(prompts, heads_axis, row_count, block_width)
    key_cache = jnp.where(inside[:, :, None], key_part, jnp.zeros_like(key_part))
    value_cache = jnp.where(inside[:, :, None], value_part, jnp.zeros_like(value_part))
    context_blocks = jnp.transpose(context, (1, 0, 2, 3))
    context_blocks = lax.all_to_all(context_blocks, "head", 0, 0, tiled=True)
    proj_blocks = proj_weight_t.reshape(model_width, heads_axis, block_width)
    attn_blocks = jnp.einsum(
        "sprf,esf->spre", context_blocks, proj_blocks, preferred_element_type=jnp.float32
    ).astype(jnp.bfloat16)
    attn_rows = jnp.sum(attn_blocks.astype(jnp.float32), axis=0)
    token_rows = lax.dynamic_slice_in_dim(tokens, row_start, row_count, 1)
    normed_rows = layer_norm(
        token_rows.astype(jnp.float32) + attn_rows, norm_gain[0], norm_shift[0]
    ).astype(jnp.bfloat16)
    hidden = jax.nn.gelu(
        jnp.einsum("pld,cdf->plcf", normed_rows, up_weight,
                   preferred_element_type=jnp.float32).reshape(prompts, row_count, hidden_width),
        approximate=False,
    ).astype(jnp.bfloat16)
    hidden = hidden.reshape(prompts, row_count, heads_axis, hidden_block)
    down_blocks = down_weight_t.reshape(model_width, heads_axis, hidden_block)
    mlp_blocks = jnp.einsum(
        "plbf,ebf->plbe", hidden, down_blocks, preferred_element_type=jnp.float32
    ).astype(jnp.bfloat16)
    mlp_rows = jnp.sum(mlp_blocks.astype(jnp.float32), axis=2)
    finished = layer_norm(normed_rows.astype(jnp.float32) + mlp_rows, norm_gain[1], norm_shift[1])
    inside_rows = lax.dynamic_slice_in_dim(inside, row_start, row_count, 1)
    encoded = jnp.where(inside_rows[:, :, None], finished, 0.0).astype(jnp.bfloat16)
    return encoded, key_cache, value_cache


def shards(tokens, lengths, attn_in, attn_out, mlp_in, mlp_out, norm_gain, norm_shift):
    heads_axis = lax.axis_size("head")
    head_index = lax.axis_index("head")
    qkv_weight, proj_weight_t, up_weight, down_weight_t = regroup_weights(
        attn_in, attn_out, mlp_in, mlp_out, heads_axis, lax.axis_size("seq"))
    prompts = tokens.shape[0]
    chunk = max(1, prompts // CHUNKS)
    pieces = []
    for lower in range(0, prompts, chunk):
        pieces.append(encode_chunk(
            tokens[lower:lower + chunk], lengths[lower:lower + chunk], qkv_weight,
            proj_weight_t, up_weight, down_weight_t, norm_gain, norm_shift,
            heads_axis, head_index))
    return tuple(jnp.concatenate(parts, axis=0) for parts in zip(*pieces))


def solution(mesh):
    in_specs = (
        P("seq", None, None),
        P("seq"),
        P(("seq", "head"), None, None),
        P(None, ("seq", "head")),
        P(("seq", "head"), None),
        P(None, ("seq", "head")),
        P(),
        P(),
    )
    out_specs = (P("seq", "head", None), P("seq", None, "head"), P("seq", None, "head"))
    return jax.shard_map(shards, mesh=mesh, in_specs=in_specs, out_specs=out_specs, check_vma=False)
```

```python
import math

import jax
import jax.numpy as jnp
from jax import lax
from jax.sharding import PartitionSpec as P

DH = 64


EPSILON = 1e-05
CHUNKS = 1


def layer_norm(values, gain, shift):
    center = values - jnp.mean(values, axis=-1, keepdims=True)
    spread = jnp.mean(center * center, axis=-1, keepdims=True)
    return center * lax.rsqrt(spread + EPSILON) * gain + shift


def regroup_weights(attn_in, attn_out, mlp_in, mlp_out, heads_axis, seq_axis):
    rows = attn_in.shape[0]
    model_width = attn_in.shape[2]
    hidden_width = mlp_in.shape[1]
    block_width = model_width // heads_axis
    in_piece = attn_in.astype(jnp.bfloat16).reshape(rows, 3, heads_axis, block_width)
    in_piece = jnp.transpose(in_piece, (0, 2, 1, 3)).reshape(rows, heads_axis, 3 * block_width)
    whole_rows = jnp.concatenate(
        [attn_out.astype(jnp.bfloat16).T, mlp_in.astype(jnp.bfloat16),
         mlp_out.astype(jnp.bfloat16).T], axis=1)
    whole_piece = jnp.broadcast_to(whole_rows[:, None], (rows, heads_axis, whole_rows.shape[1]))
    packed = jnp.concatenate([in_piece, whole_piece], axis=2)
    packed = lax.all_to_all(packed, "head", 1, 0, tiled=True)
    packed = packed.reshape(rows * heads_axis, packed.shape[2])
    in_part = packed[:, :3 * block_width]
    in_part = jnp.broadcast_to(in_part[None], (seq_axis,) + in_part.shape)
    qkv_weight = lax.all_to_all(in_part, "seq", 0, 0, tiled=True)
    qkv_weight = qkv_weight.reshape(-1, 3, block_width)
    early_end = 3 * block_width + model_width + hidden_width
    early = lax.all_gather(packed[:, 3 * block_width:early_end], "seq", axis=0, tiled=True)
    proj_weight_t = early[:, :model_width]
    up_weight = early[:, model_width:]
    down_weight_t = lax.all_gather(packed[:, early_end:], "seq", axis=0, tiled=True)
    return qkv_weight, proj_weight_t, up_weight, down_weight_t


def encode_chunk(tokens, lengths, qkv_weight, proj_weight_t, up_weight, down_weight_t,
                 norm_gain, norm_shift, heads_axis, head_index):
    prompts = tokens.shape[0]
    seq_len = tokens.shape[1]
    model_width = tokens.shape[2]
    hidden_width = up_weight.shape[1]
    block_width = model_width // heads_axis
    hidden_block = hidden_width // heads_axis
    local_heads = block_width // DH
    row_count = seq_len // heads_axis
    row_start = head_index * row_count
    projected = jnp.einsum(
        "pld,dte->plte", tokens, qkv_weight, preferred_element_type=jnp.float32
    ).astype(jnp.bfloat16)
    positions = jnp.arange(seq_len, dtype=jnp.int32)
    inside = positions[None, :] < lengths[:, None]
    key_part = projected[:, :, 1]
    value_part = projected[:, :, 2]
    queries = projected[:, :, 0].reshape(prompts, seq_len, local_heads, DH)
    key_heads = key_part.reshape(prompts, seq_len, local_heads, DH)
    value_heads = value_part.reshape(prompts, seq_len, local_heads, DH)
    scores = jnp.einsum(
        "pqhd,pkhd->phqk", queries, key_heads, preferred_element_type=jnp.float32
    ) * (1.0 / math.sqrt(DH))
    scores = jnp.where(inside[:, None, None, :], scores, -1e30)
    row_peak = jnp.max(scores, axis=-1, keepdims=True)
    raised = jnp.exp(scores - row_peak)
    weights = (raised / jnp.sum(raised, axis=-1, keepdims=True)).astype(jnp.bfloat16)
    context = jnp.einsum(
        "phqk,pkhd->pqhd", weights, value_heads, preferred_element_type=jnp.float32
    )
    context = context.astype(jnp.bfloat16).reshape(prompts, heads_axis, row_count, block_width)
    key_cache = jnp.where(inside[:, :, None], key_part, jnp.zeros_like(key_part))
    value_cache = jnp.where(inside[:, :, None], value_part, jnp.zeros_like(value_part))
    context_blocks = jnp.transpose(context, (1, 0, 2, 3))
    context_blocks = lax.all_to_all(context_blocks, "head", 0, 0, tiled=True)
    proj_blocks = proj_weight_t.reshape(model_width, heads_axis, block_width)
    attn_blocks = jnp.einsum(
        "sprf,esf->spre", context_blocks, proj_blocks, preferred_element_type=jnp.float32
    ).astype(jnp.bfloat16)
    attn_rows = jnp.sum(attn_blocks.astype(jnp.float32), axis=0)
    token_rows = lax.dynamic_slice_in_dim(tokens, row_start, row_count, 1)
    normed_rows = layer_norm(
        token_rows.astype(jnp.float32) + attn_rows, norm_gain[0], norm_shift[0]
    ).astype(jnp.bfloat16)
    hidden = jax.nn.gelu(
        jnp.einsum("pld,df->plf", normed_rows, up_weight, preferred_element_type=jnp.float32),
        approximate=False,
    ).astype(jnp.bfloat16)
    hidden = hidden.reshape(prompts, row_count, heads_axis, hidden_block)
    down_blocks = down_weight_t.reshape(model_width, heads_axis, hidden_block)
    mlp_blocks = jnp.einsum(
        "plbf,ebf->plbe", hidden, down_blocks, preferred_element_type=jnp.float32
    ).astype(jnp.bfloat16)
    mlp_rows = jnp.sum(mlp_blocks.astype(jnp.float32), axis=2)
    finished = layer_norm(normed_rows.astype(jnp.float32) + mlp_rows, norm_gain[1], norm_shift[1])
    inside_rows = lax.dynamic_slice_in_dim(inside, row_start, row_count, 1)
    encoded = jnp.where(inside_rows[:, :, None], finished, 0.0).astype(jnp.bfloat16)
    return encoded, key_cache, value_cache


def shards(tokens, lengths, attn_in, attn_out, mlp_in, mlp_out, norm_gain, norm_shift):
    heads_axis = lax.axis_size("head")
    head_index = lax.axis_index("head")
    qkv_weight, proj_weight_t, up_weight, down_weight_t = regroup_weights(
        attn_in, attn_out, mlp_in, mlp_out, heads_axis, lax.axis_size("seq"))
    prompts = tokens.shape[0]
    chunk = max(1, prompts // CHUNKS)
    pieces = []
    for lower in range(0, prompts, chunk):
        pieces.append(encode_chunk(
            tokens[lower:lower + chunk], lengths[lower:lower + chunk], qkv_weight,
            proj_weight_t, up_weight, down_weight_t, norm_gain, norm_shift,
            heads_axis, head_index))
    return tuple(jnp.concatenate(parts, axis=0) for parts in zip(*pieces))


def solution(mesh):
    in_specs = (
        P("seq", None, None),
        P("seq"),
        P(("seq", "head"), None, None),
        P(None, ("seq", "head")),
        P(("seq", "head"), None),
        P(None, ("seq", "head")),
        P(),
        P(),
    )
    out_specs = (P("seq", "head", None), P("seq", None, "head"), P("seq", None, "head"))
    return jax.shard_map(shards, mesh=mesh, in_specs=in_specs, out_specs=out_specs, check_vma=False)
```

```python
import math

import jax
import jax.numpy as jnp
from jax import lax
from jax.sharding import PartitionSpec as P

DH = 64


EPSILON = 1e-05
CHUNKS = 1


def layer_norm(values, gain, shift):
    center = values - jnp.mean(values, axis=-1, keepdims=True)
    spread = jnp.mean(center * center, axis=-1, keepdims=True)
    return center * lax.rsqrt(spread + EPSILON) * gain + shift


def regroup_weights(attn_in, attn_out, mlp_in, mlp_out, heads_axis, seq_axis):
    rows = attn_in.shape[0]
    model_width = attn_in.shape[2]
    hidden_width = mlp_in.shape[1]
    block_width = model_width // heads_axis
    in_piece = attn_in.astype(jnp.bfloat16).reshape(rows, 3, heads_axis, block_width)
    in_piece = jnp.transpose(in_piece, (0, 2, 1, 3)).reshape(rows, heads_axis, 3 * block_width)
    whole_rows = jnp.concatenate(
        [attn_out.astype(jnp.bfloat16).T, mlp_in.astype(jnp.bfloat16),
         mlp_out.astype(jnp.bfloat16).T], axis=1)
    whole_piece = jnp.broadcast_to(whole_rows[:, None], (rows, heads_axis, whole_rows.shape[1]))
    packed = jnp.concatenate([in_piece, whole_piece], axis=2)
    packed = lax.all_to_all(packed, "head", 1, 0, tiled=True)
    packed = packed.reshape(rows * heads_axis, packed.shape[2])
    in_part = packed[:, :3 * block_width]
    in_part = jnp.broadcast_to(in_part[None], (seq_axis,) + in_part.shape)
    qkv_weight = lax.all_to_all(in_part, "seq", 0, 0, tiled=True)
    qkv_weight = qkv_weight.reshape(-1, 3, block_width)
    early_end = 3 * block_width + model_width + hidden_width
    early = lax.all_gather(packed[:, 3 * block_width:early_end], "seq", axis=0, tiled=True)
    proj_weight_t = early[:, :model_width]
    up_weight = early[:, model_width:]
    down_weight_t = lax.all_gather(packed[:, early_end:], "seq", axis=0, tiled=True)
    return qkv_weight, proj_weight_t, up_weight, down_weight_t


def encode_chunk(tokens, lengths, qkv_weight, proj_weight_t, up_weight, down_weight_t,
                 norm_gain, norm_shift, heads_axis, head_index):
    prompts = tokens.shape[0]
    seq_len = tokens.shape[1]
    model_width = tokens.shape[2]
    hidden_width = up_weight.shape[1]
    block_width = model_width // heads_axis
    hidden_block = hidden_width // heads_axis
    local_heads = block_width // DH
    row_count = seq_len // heads_axis
    row_start = head_index * row_count
    projected = jnp.einsum(
        "pld,dte->plte", tokens, qkv_weight, preferred_element_type=jnp.float32
    ).astype(jnp.bfloat16)
    positions = jnp.arange(seq_len, dtype=jnp.int32)
    inside = positions[None, :] < lengths[:, None]
    key_part = projected[:, :, 1]
    value_part = projected[:, :, 2]
    queries = projected[:, :, 0].reshape(prompts, seq_len, local_heads, DH)
    key_heads = key_part.reshape(prompts, seq_len, local_heads, DH)
    value_heads = value_part.reshape(prompts, seq_len, local_heads, DH)
    scores = jnp.einsum(
        "pqhd,pkhd->phqk", queries, key_heads, preferred_element_type=jnp.float32
    ) * (1.0 / math.sqrt(DH))
    scores = jnp.where(inside[:, None, None, :], scores, -1e30)
    row_peak = jnp.max(scores, axis=-1, keepdims=True)
    raised = jnp.exp(scores - row_peak)
    weights = (raised / jnp.sum(raised, axis=-1, keepdims=True)).astype(jnp.bfloat16)
    weights = weights.reshape(prompts, local_heads, heads_axis, row_count, seq_len)
    context = jnp.einsum(
        "phjrk,pkhd->jprhd", weights, value_heads, preferred_element_type=jnp.float32
    )
    context_blocks = context.astype(jnp.bfloat16).reshape(
        heads_axis, prompts, row_count, block_width)
    key_cache = jnp.where(inside[:, :, None], key_part, jnp.zeros_like(key_part))
    value_cache = jnp.where(inside[:, :, None], value_part, jnp.zeros_like(value_part))
    context_blocks = lax.all_to_all(context_blocks, "head", 0, 0, tiled=True)
    proj_blocks = proj_weight_t.reshape(model_width, heads_axis, block_width)
    attn_blocks = jnp.einsum(
        "sprf,esf->spre", context_blocks, proj_blocks, preferred_element_type=jnp.float32
    ).astype(jnp.bfloat16)
    attn_rows = jnp.sum(attn_blocks.astype(jnp.float32), axis=0)
    token_rows = lax.dynamic_slice_in_dim(tokens, row_start, row_count, 1)
    normed_rows = layer_norm(
        token_rows.astype(jnp.float32) + attn_rows, norm_gain[0], norm_shift[0]
    ).astype(jnp.bfloat16)
    hidden = jax.nn.gelu(
        jnp.einsum("pld,df->plf", normed_rows, up_weight, preferred_element_type=jnp.float32),
        approximate=False,
    ).astype(jnp.bfloat16)
    hidden = hidden.reshape(prompts, row_count, heads_axis, hidden_block)
    down_blocks = down_weight_t.reshape(model_width, heads_axis, hidden_block)
    mlp_blocks = jnp.einsum(
        "plbf,ebf->plbe", hidden, down_blocks, preferred_element_type=jnp.float32
    ).astype(jnp.bfloat16)
    mlp_rows = jnp.sum(mlp_blocks.astype(jnp.float32), axis=2)
    finished = layer_norm(normed_rows.astype(jnp.float32) + mlp_rows, norm_gain[1], norm_shift[1])
    inside_rows = lax.dynamic_slice_in_dim(inside, row_start, row_count, 1)
    encoded = jnp.where(inside_rows[:, :, None], finished, 0.0).astype(jnp.bfloat16)
    return encoded, key_cache, value_cache


def shards(tokens, lengths, attn_in, attn_out, mlp_in, mlp_out, norm_gain, norm_shift):
    heads_axis = lax.axis_size("head")
    head_index = lax.axis_index("head")
    qkv_weight, proj_weight_t, up_weight, down_weight_t = regroup_weights(
        attn_in, attn_out, mlp_in, mlp_out, heads_axis, lax.axis_size("seq"))
    prompts = tokens.shape[0]
    chunk = max(1, prompts // CHUNKS)
    pieces = []
    for lower in range(0, prompts, chunk):
        pieces.append(encode_chunk(
            tokens[lower:lower + chunk], lengths[lower:lower + chunk], qkv_weight,
            proj_weight_t, up_weight, down_weight_t, norm_gain, norm_shift,
            heads_axis, head_index))
    return tuple(jnp.concatenate(parts, axis=0) for parts in zip(*pieces))


def solution(mesh):
    in_specs = (
        P("seq", None, None),
        P("seq"),
        P(("seq", "head"), None, None),
        P(None, ("seq", "head")),
        P(("seq", "head"), None),
        P(None, ("seq", "head")),
        P(),
        P(),
    )
    out_specs = (P("seq", "head", None), P("seq", None, "head"), P("seq", None, "head"))
    return jax.shard_map(shards, mesh=mesh, in_specs=in_specs, out_specs=out_specs, check_vma=False)
```

```python
import math

import jax
import jax.numpy as jnp
from jax import lax
from jax.sharding import PartitionSpec as P

DH = 64


EPSILON = 1e-05
CHUNKS = 1


def layer_norm(values, gain, shift):
    center = values - jnp.mean(values, axis=-1, keepdims=True)
    spread = jnp.mean(center * center, axis=-1, keepdims=True)
    return center * lax.rsqrt(spread + EPSILON) * gain + shift


def regroup_weights(attn_in, attn_out, mlp_in, mlp_out, heads_axis, seq_axis):
    rows = attn_in.shape[0]
    model_width = attn_in.shape[2]
    hidden_width = mlp_in.shape[1]
    block_width = model_width // heads_axis
    in_piece = attn_in.astype(jnp.bfloat16).reshape(rows, 3, heads_axis, block_width)
    in_piece = jnp.transpose(in_piece, (0, 2, 1, 3)).reshape(rows, heads_axis, 3 * block_width)
    whole_rows = jnp.concatenate(
        [attn_out.astype(jnp.bfloat16).T, mlp_in.astype(jnp.bfloat16),
         mlp_out.astype(jnp.bfloat16).T], axis=1)
    whole_piece = jnp.broadcast_to(whole_rows[:, None], (rows, heads_axis, whole_rows.shape[1]))
    whole_piece = lax.all_to_all(whole_piece, "head", 1, 0, tiled=True)
    whole_piece = whole_piece.reshape(rows * heads_axis, whole_piece.shape[2])
    in_piece, whole_piece = lax.optimization_barrier((in_piece, whole_piece))
    in_part = lax.all_to_all(in_piece, "head", 1, 0, tiled=True)
    in_part = in_part.reshape(rows * heads_axis, 3 * block_width)
    in_part = jnp.broadcast_to(in_part[None], (seq_axis,) + in_part.shape)
    qkv_weight = lax.all_to_all(in_part, "seq", 0, 0, tiled=True)
    qkv_weight = qkv_weight.reshape(-1, 3, block_width)
    packed = whole_piece
    early_end = model_width + hidden_width
    early = lax.all_gather(packed[:, :early_end], "seq", axis=0, tiled=True)
    proj_weight_t = early[:, :model_width]
    up_weight = early[:, model_width:]
    down_weight_t = lax.all_gather(packed[:, early_end:], "seq", axis=0, tiled=True)
    return qkv_weight, proj_weight_t, up_weight, down_weight_t


def encode_chunk(tokens, lengths, qkv_weight, proj_weight_t, up_weight, down_weight_t,
                 norm_gain, norm_shift, heads_axis, head_index):
    prompts = tokens.shape[0]
    seq_len = tokens.shape[1]
    model_width = tokens.shape[2]
    hidden_width = up_weight.shape[1]
    block_width = model_width // heads_axis
    hidden_block = hidden_width // heads_axis
    local_heads = block_width // DH
    row_count = seq_len // heads_axis
    row_start = head_index * row_count
    projected = jnp.einsum(
        "pld,dte->plte", tokens, qkv_weight, preferred_element_type=jnp.float32
    ).astype(jnp.bfloat16)
    positions = jnp.arange(seq_len, dtype=jnp.int32)
    inside = positions[None, :] < lengths[:, None]
    key_part = projected[:, :, 1]
    value_part = projected[:, :, 2]
    queries = projected[:, :, 0].reshape(prompts, seq_len, local_heads, DH)
    key_heads = key_part.reshape(prompts, seq_len, local_heads, DH)
    value_heads = value_part.reshape(prompts, seq_len, local_heads, DH)
    scores = jnp.einsum(
        "pqhd,pkhd->phqk", queries, key_heads, preferred_element_type=jnp.float32
    ) * (1.0 / math.sqrt(DH))
    scores = jnp.where(inside[:, None, None, :], scores, -1e30)
    row_peak = jnp.max(scores, axis=-1, keepdims=True)
    raised = jnp.exp(scores - row_peak)
    weights = (raised / jnp.sum(raised, axis=-1, keepdims=True)).astype(jnp.bfloat16)
    context = jnp.einsum(
        "phqk,pkhd->pqhd", weights, value_heads, preferred_element_type=jnp.float32
    )
    context = context.astype(jnp.bfloat16).reshape(prompts, heads_axis, row_count, block_width)
    key_cache = jnp.where(inside[:, :, None], key_part, jnp.zeros_like(key_part))
    value_cache = jnp.where(inside[:, :, None], value_part, jnp.zeros_like(value_part))
    context_blocks = jnp.transpose(context, (1, 0, 2, 3))
    context_blocks = lax.all_to_all(context_blocks, "head", 0, 0, tiled=True)
    proj_blocks = proj_weight_t.reshape(model_width, heads_axis, block_width)
    attn_blocks = jnp.einsum(
        "sprf,esf->spre", context_blocks, proj_blocks, preferred_element_type=jnp.float32
    ).astype(jnp.bfloat16)
    attn_rows = jnp.sum(attn_blocks.astype(jnp.float32), axis=0)
    token_rows = lax.dynamic_slice_in_dim(tokens, row_start, row_count, 1)
    normed_rows = layer_norm(
        token_rows.astype(jnp.float32) + attn_rows, norm_gain[0], norm_shift[0]
    ).astype(jnp.bfloat16)
    hidden = jax.nn.gelu(
        jnp.einsum("pld,df->plf", normed_rows, up_weight, preferred_element_type=jnp.float32),
        approximate=False,
    ).astype(jnp.bfloat16)
    hidden = hidden.reshape(prompts, row_count, heads_axis, hidden_block)
    down_blocks = down_weight_t.reshape(model_width, heads_axis, hidden_block)
    mlp_blocks = jnp.einsum(
        "plbf,ebf->plbe", hidden, down_blocks, preferred_element_type=jnp.float32
    ).astype(jnp.bfloat16)
    mlp_rows = jnp.sum(mlp_blocks.astype(jnp.float32), axis=2)
    finished = layer_norm(normed_rows.astype(jnp.float32) + mlp_rows, norm_gain[1], norm_shift[1])
    inside_rows = lax.dynamic_slice_in_dim(inside, row_start, row_count, 1)
    encoded = jnp.where(inside_rows[:, :, None], finished, 0.0).astype(jnp.bfloat16)
    return encoded, key_cache, value_cache


def shards(tokens, lengths, attn_in, attn_out, mlp_in, mlp_out, norm_gain, norm_shift):
    heads_axis = lax.axis_size("head")
    head_index = lax.axis_index("head")
    qkv_weight, proj_weight_t, up_weight, down_weight_t = regroup_weights(
        attn_in, attn_out, mlp_in, mlp_out, heads_axis, lax.axis_size("seq"))
    prompts = tokens.shape[0]
    chunk = max(1, prompts // CHUNKS)
    pieces = []
    for lower in range(0, prompts, chunk):
        pieces.append(encode_chunk(
            tokens[lower:lower + chunk], lengths[lower:lower + chunk], qkv_weight,
            proj_weight_t, up_weight, down_weight_t, norm_gain, norm_shift,
            heads_axis, head_index))
    return tuple(jnp.concatenate(parts, axis=0) for parts in zip(*pieces))


def solution(mesh):
    in_specs = (
        P("seq", None, None),
        P("seq"),
        P(("seq", "head"), None, None),
        P(None, ("seq", "head")),
        P(("seq", "head"), None),
        P(None, ("seq", "head")),
        P(),
        P(),
    )
    out_specs = (P("seq", "head", None), P("seq", None, "head"), P("seq", None, "head"))
    return jax.shard_map(shards, mesh=mesh, in_specs=in_specs, out_specs=out_specs, check_vma=False)
```

```python
import math

import functools

import jax
import jax.numpy as jnp
from jax import lax
from jax.experimental import pallas as pl
from jax.experimental.pallas import tpu as pltpu
from jax.sharding import PartitionSpec as P

DH = 64


EPSILON = 1e-05
CHUNKS = 1


def layer_norm(values, gain, shift):
    center = values - jnp.mean(values, axis=-1, keepdims=True)
    spread = jnp.mean(center * center, axis=-1, keepdims=True)
    return center * lax.rsqrt(spread + EPSILON) * gain + shift


def exchange_kernel(n, x_ref, y_ref, send_sems, recv_sems, local_sem):
    me = lax.axis_index("head")
    s = lax.axis_index("seq")
    mesh_ids = pl.DeviceIdType.MESH
    barrier = pltpu.get_barrier_semaphore()
    for j in range(1, n):
        pl.semaphore_signal(barrier, inc=1, device_id=(s, lax.rem(me + j, n)),
                            device_id_type=mesh_ids)
    pl.semaphore_wait(barrier, n - 1)
    local = pltpu.make_async_copy(x_ref.at[me], y_ref.at[me], local_sem)
    local.start()
    copies = []
    for j in range(1, n):
        peer = lax.rem(me + j, n)
        copy = pltpu.make_async_remote_copy(
            src_ref=x_ref.at[peer], dst_ref=y_ref.at[me],
            send_sem=send_sems.at[j], recv_sem=recv_sems.at[j],
            device_id=(s, peer), device_id_type=mesh_ids)
        copy.start()
        copies.append(copy)
    local.wait()
    for j in range(1, n):
        origin = lax.rem(me + n - j, n)
        copies[j - 1].wait_send()
        incoming = pltpu.make_async_remote_copy(
            src_ref=x_ref.at[origin], dst_ref=y_ref.at[origin],
            send_sem=send_sems.at[j], recv_sem=recv_sems.at[j],
            device_id=(s, origin), device_id_type=mesh_ids)
        incoming.wait_recv()


def exchange(x, n):
    return pl.pallas_call(
        functools.partial(exchange_kernel, n),
        out_shape=jax.ShapeDtypeStruct(x.shape, x.dtype),
        in_specs=[pl.BlockSpec(memory_space=pl.ANY)],
        out_specs=pl.BlockSpec(memory_space=pl.ANY),
        scratch_shapes=[pltpu.SemaphoreType.DMA((n,)), pltpu.SemaphoreType.DMA((n,)),
                        pltpu.SemaphoreType.DMA(())],
        compiler_params=pltpu.CompilerParams(collective_id=0, has_side_effects=True),
    )(x)


def regroup_weights(attn_in, attn_out, mlp_in, mlp_out, heads_axis, seq_axis):
    rows = attn_in.shape[0]
    model_width = attn_in.shape[2]
    hidden_width = mlp_in.shape[1]
    block_width = model_width // heads_axis
    in_piece = attn_in.astype(jnp.bfloat16).reshape(rows, 3, heads_axis, block_width)
    in_piece = jnp.transpose(in_piece, (0, 2, 1, 3)).reshape(rows, heads_axis, 3 * block_width)
    whole_rows = jnp.concatenate(
        [attn_out.astype(jnp.bfloat16).T, mlp_in.astype(jnp.bfloat16),
         mlp_out.astype(jnp.bfloat16).T], axis=1)
    whole_piece = jnp.broadcast_to(whole_rows[:, None], (rows, heads_axis, whole_rows.shape[1]))
    packed = jnp.concatenate([in_piece, whole_piece], axis=2)
    packed = lax.all_to_all(packed, "head", 1, 0, tiled=True)
    packed = packed.reshape(rows * heads_axis, packed.shape[2])
    in_part = packed[:, :3 * block_width]
    in_part = jnp.broadcast_to(in_part[None], (seq_axis,) + in_part.shape)
    qkv_weight = lax.all_to_all(in_part, "seq", 0, 0, tiled=True)
    qkv_weight = qkv_weight.reshape(-1, 3, block_width)
    early_end = 3 * block_width + model_width + hidden_width
    early = lax.all_gather(packed[:, 3 * block_width:early_end], "seq", axis=0, tiled=True)
    proj_weight_t = early[:, :model_width]
    up_weight = early[:, model_width:]
    down_weight_t = lax.all_gather(packed[:, early_end:], "seq", axis=0, tiled=True)
    return qkv_weight, proj_weight_t, up_weight, down_weight_t


def encode_chunk(tokens, lengths, qkv_weight, proj_weight_t, up_weight, down_weight_t,
                 norm_gain, norm_shift, heads_axis, head_index):
    prompts = tokens.shape[0]
    seq_len = tokens.shape[1]
    model_width = tokens.shape[2]
    hidden_width = up_weight.shape[1]
    block_width = model_width // heads_axis
    hidden_block = hidden_width // heads_axis
    local_heads = block_width // DH
    row_count = seq_len // heads_axis
    row_start = head_index * row_count
    projected = jnp.einsum(
        "pld,dte->plte", tokens, qkv_weight, preferred_element_type=jnp.float32
    ).astype(jnp.bfloat16)
    positions = jnp.arange(seq_len, dtype=jnp.int32)
    inside = positions[None, :] < lengths[:, None]
    key_part = projected[:, :, 1]
    value_part = projected[:, :, 2]
    queries = projected[:, :, 0].reshape(prompts, seq_len, local_heads, DH)
    key_heads = key_part.reshape(prompts, seq_len, local_heads, DH)
    value_heads = value_part.reshape(prompts, seq_len, local_heads, DH)
    scores = jnp.einsum(
        "pqhd,pkhd->phqk", queries, key_heads, preferred_element_type=jnp.float32
    ) * (1.0 / math.sqrt(DH))
    scores = jnp.where(inside[:, None, None, :], scores, -1e30)
    row_peak = jnp.max(scores, axis=-1, keepdims=True)
    raised = jnp.exp(scores - row_peak)
    weights = (raised / jnp.sum(raised, axis=-1, keepdims=True)).astype(jnp.bfloat16)
    context = jnp.einsum(
        "phqk,pkhd->pqhd", weights, value_heads, preferred_element_type=jnp.float32
    )
    context = context.astype(jnp.bfloat16).reshape(prompts, heads_axis, row_count, block_width)
    key_cache = jnp.where(inside[:, :, None], key_part, jnp.zeros_like(key_part))
    value_cache = jnp.where(inside[:, :, None], value_part, jnp.zeros_like(value_part))
    context_blocks = jnp.transpose(context, (1, 0, 2, 3))
    context_blocks = exchange(context_blocks, heads_axis)
    proj_blocks = proj_weight_t.reshape(model_width, heads_axis, block_width)
    attn_blocks = jnp.einsum(
        "sprf,esf->spre", context_blocks, proj_blocks, preferred_element_type=jnp.float32
    ).astype(jnp.bfloat16)
    attn_rows = jnp.sum(attn_blocks.astype(jnp.float32), axis=0)
    token_rows = lax.dynamic_slice_in_dim(tokens, row_start, row_count, 1)
    normed_rows = layer_norm(
        token_rows.astype(jnp.float32) + attn_rows, norm_gain[0], norm_shift[0]
    ).astype(jnp.bfloat16)
    hidden = jax.nn.gelu(
        jnp.einsum("pld,df->plf", normed_rows, up_weight, preferred_element_type=jnp.float32),
        approximate=False,
    ).astype(jnp.bfloat16)
    hidden = hidden.reshape(prompts, row_count, heads_axis, hidden_block)
    down_blocks = down_weight_t.reshape(model_width, heads_axis, hidden_block)
    mlp_blocks = jnp.einsum(
        "plbf,ebf->plbe", hidden, down_blocks, preferred_element_type=jnp.float32
    ).astype(jnp.bfloat16)
    mlp_rows = jnp.sum(mlp_blocks.astype(jnp.float32), axis=2)
    finished = layer_norm(normed_rows.astype(jnp.float32) + mlp_rows, norm_gain[1], norm_shift[1])
    inside_rows = lax.dynamic_slice_in_dim(inside, row_start, row_count, 1)
    encoded = jnp.where(inside_rows[:, :, None], finished, 0.0).astype(jnp.bfloat16)
    return encoded, key_cache, value_cache


def shards(tokens, lengths, attn_in, attn_out, mlp_in, mlp_out, norm_gain, norm_shift):
    heads_axis = lax.axis_size("head")
    head_index = lax.axis_index("head")
    qkv_weight, proj_weight_t, up_weight, down_weight_t = regroup_weights(
        attn_in, attn_out, mlp_in, mlp_out, heads_axis, lax.axis_size("seq"))
    prompts = tokens.shape[0]
    chunk = max(1, prompts // CHUNKS)
    pieces = []
    for lower in range(0, prompts, chunk):
        pieces.append(encode_chunk(
            tokens[lower:lower + chunk], lengths[lower:lower + chunk], qkv_weight,
            proj_weight_t, up_weight, down_weight_t, norm_gain, norm_shift,
            heads_axis, head_index))
    return tuple(jnp.concatenate(parts, axis=0) for parts in zip(*pieces))


def solution(mesh):
    in_specs = (
        P("seq", None, None),
        P("seq"),
        P(("seq", "head"), None, None),
        P(None, ("seq", "head")),
        P(("seq", "head"), None),
        P(None, ("seq", "head")),
        P(),
        P(),
    )
    out_specs = (P("seq", "head", None), P("seq", None, "head"), P("seq", None, "head"))
    return jax.shard_map(shards, mesh=mesh, in_specs=in_specs, out_specs=out_specs, check_vma=False)
```

```python
import math

import jax
import jax.numpy as jnp
from jax import lax
from jax.sharding import PartitionSpec as P

DH = 64


EPSILON = 1e-05
CHUNKS = 1


def layer_norm(values, gain, shift):
    center = values - jnp.mean(values, axis=-1, keepdims=True)
    spread = jnp.mean(center * center, axis=-1, keepdims=True)
    return center * lax.rsqrt(spread + EPSILON) * gain + shift


def regroup_weights(attn_in, attn_out, mlp_in, mlp_out, heads_axis, seq_axis):
    rows = attn_in.shape[0]
    model_width = attn_in.shape[2]
    hidden_width = mlp_in.shape[1]
    block_width = model_width // heads_axis
    in_piece = attn_in.astype(jnp.bfloat16).reshape(rows, 3, heads_axis, block_width)
    in_piece = jnp.transpose(in_piece, (0, 2, 1, 3)).reshape(rows, heads_axis, 3 * block_width)
    whole_rows = jnp.concatenate(
        [attn_out.astype(jnp.bfloat16).T, mlp_in.astype(jnp.bfloat16),
         mlp_out.astype(jnp.bfloat16).T], axis=1)
    whole_piece = jnp.broadcast_to(whole_rows[:, None], (rows, heads_axis, whole_rows.shape[1]))
    packed = jnp.concatenate([in_piece, whole_piece], axis=2)
    packed = lax.all_to_all(packed, "head", 1, 0, tiled=True)
    packed = packed.reshape(rows * heads_axis, packed.shape[2])
    in_part = packed[:, :3 * block_width]
    in_part = jnp.broadcast_to(in_part[None], (seq_axis,) + in_part.shape)
    qkv_weight = lax.all_to_all(in_part, "seq", 0, 0, tiled=True)
    qkv_weight = qkv_weight.reshape(-1, 3, block_width)
    early_end = 3 * block_width + model_width + hidden_width
    early = lax.all_gather(packed[:, 3 * block_width:early_end], "seq", axis=0, tiled=True)
    proj_weight_t = early[:, :model_width]
    up_weight = early[:, model_width:]
    half = hidden_width // 2
    down_weight_t = tuple(
        lax.all_gather(packed[:, lower:lower + half], "seq", axis=0, tiled=True)
        for lower in (early_end, early_end + half))
    return qkv_weight, proj_weight_t, up_weight, down_weight_t


def encode_chunk(tokens, lengths, qkv_weight, proj_weight_t, up_weight, down_weight_t,
                 norm_gain, norm_shift, heads_axis, head_index):
    prompts = tokens.shape[0]
    seq_len = tokens.shape[1]
    model_width = tokens.shape[2]
    hidden_width = up_weight.shape[1]
    block_width = model_width // heads_axis
    hidden_block = hidden_width // heads_axis
    local_heads = block_width // DH
    row_count = seq_len // heads_axis
    row_start = head_index * row_count
    projected = jnp.einsum(
        "pld,dte->plte", tokens, qkv_weight, preferred_element_type=jnp.float32
    ).astype(jnp.bfloat16)
    positions = jnp.arange(seq_len, dtype=jnp.int32)
    inside = positions[None, :] < lengths[:, None]
    key_part = projected[:, :, 1]
    value_part = projected[:, :, 2]
    queries = projected[:, :, 0].reshape(prompts, seq_len, local_heads, DH)
    key_heads = key_part.reshape(prompts, seq_len, local_heads, DH)
    value_heads = value_part.reshape(prompts, seq_len, local_heads, DH)
    scores = jnp.einsum(
        "pqhd,pkhd->phqk", queries, key_heads, preferred_element_type=jnp.float32
    ) * (1.0 / math.sqrt(DH))
    scores = jnp.where(inside[:, None, None, :], scores, -1e30)
    row_peak = jnp.max(scores, axis=-1, keepdims=True)
    raised = jnp.exp(scores - row_peak)
    weights = (raised / jnp.sum(raised, axis=-1, keepdims=True)).astype(jnp.bfloat16)
    context = jnp.einsum(
        "phqk,pkhd->pqhd", weights, value_heads, preferred_element_type=jnp.float32
    )
    context = context.astype(jnp.bfloat16).reshape(prompts, heads_axis, row_count, block_width)
    key_cache = jnp.where(inside[:, :, None], key_part, jnp.zeros_like(key_part))
    value_cache = jnp.where(inside[:, :, None], value_part, jnp.zeros_like(value_part))
    context_blocks = jnp.transpose(context, (1, 0, 2, 3))
    context_blocks = lax.all_to_all(context_blocks, "head", 0, 0, tiled=True)
    proj_blocks = proj_weight_t.reshape(model_width, heads_axis, block_width)
    attn_blocks = jnp.einsum(
        "sprf,esf->spre", context_blocks, proj_blocks, preferred_element_type=jnp.float32
    ).astype(jnp.bfloat16)
    attn_rows = jnp.sum(attn_blocks.astype(jnp.float32), axis=0)
    token_rows = lax.dynamic_slice_in_dim(tokens, row_start, row_count, 1)
    normed_rows = layer_norm(
        token_rows.astype(jnp.float32) + attn_rows, norm_gain[0], norm_shift[0]
    ).astype(jnp.bfloat16)
    hidden = jax.nn.gelu(
        jnp.einsum("pld,df->plf", normed_rows, up_weight, preferred_element_type=jnp.float32),
        approximate=False,
    ).astype(jnp.bfloat16)
    half_blocks = heads_axis // 2
    hidden = hidden.reshape(prompts, row_count, 2, half_blocks, hidden_block)
    mlp_rows = None
    for part, down_half in enumerate(down_weight_t):
        if mlp_rows is not None:
            mlp_rows, down_half = lax.optimization_barrier((mlp_rows, down_half))
        half_blocks_out = jnp.einsum(
            "plbf,ebf->plbe", hidden[:, :, part],
            down_half.reshape(model_width, half_blocks, hidden_block),
            preferred_element_type=jnp.float32,
        ).astype(jnp.bfloat16)
        half_rows = jnp.sum(half_blocks_out.astype(jnp.float32), axis=2)
        mlp_rows = half_rows if mlp_rows is None else mlp_rows + half_rows
    finished = layer_norm(normed_rows.astype(jnp.float32) + mlp_rows, norm_gain[1], norm_shift[1])
    inside_rows = lax.dynamic_slice_in_dim(inside, row_start, row_count, 1)
    encoded = jnp.where(inside_rows[:, :, None], finished, 0.0).astype(jnp.bfloat16)
    return encoded, key_cache, value_cache


def shards(tokens, lengths, attn_in, attn_out, mlp_in, mlp_out, norm_gain, norm_shift):
    heads_axis = lax.axis_size("head")
    head_index = lax.axis_index("head")
    qkv_weight, proj_weight_t, up_weight, down_weight_t = regroup_weights(
        attn_in, attn_out, mlp_in, mlp_out, heads_axis, lax.axis_size("seq"))
    prompts = tokens.shape[0]
    chunk = max(1, prompts // CHUNKS)
    pieces = []
    for lower in range(0, prompts, chunk):
        pieces.append(encode_chunk(
            tokens[lower:lower + chunk], lengths[lower:lower + chunk], qkv_weight,
            proj_weight_t, up_weight, down_weight_t, norm_gain, norm_shift,
            heads_axis, head_index))
    return tuple(jnp.concatenate(parts, axis=0) for parts in zip(*pieces))


def solution(mesh):
    in_specs = (
        P("seq", None, None),
        P("seq"),
        P(("seq", "head"), None, None),
        P(None, ("seq", "head")),
        P(("seq", "head"), None),
        P(None, ("seq", "head")),
        P(),
        P(),
    )
    out_specs = (P("seq", "head", None), P("seq", None, "head"), P("seq", None, "head"))
    return jax.shard_map(shards, mesh=mesh, in_specs=in_specs, out_specs=out_specs, check_vma=False)
```

```python
import math

import jax
import jax.numpy as jnp
from jax import lax
from jax.sharding import PartitionSpec as P

DH = 64


EPSILON = 1e-05
CHUNKS = 1


def layer_norm(values, gain, shift):
    center = values - jnp.mean(values, axis=-1, keepdims=True)
    spread = jnp.mean(center * center, axis=-1, keepdims=True)
    return center * lax.rsqrt(spread + EPSILON) * gain + shift


def pair_gather(part, seq_axis):
    core = lax.axis_index("seq") % 2
    low_first = core == 0
    pairs = [(index, index ^ 1) for index in range(seq_axis)]
    groups = [[index for index in range(seq_axis) if index % 2 == side] for side in range(2)]
    half = part.shape[1] // 2
    other = lax.ppermute(part, "seq", pairs)
    both = jnp.where(low_first, jnp.concatenate([part, other], 0),
                     jnp.concatenate([other, part], 0))
    mine = lax.dynamic_slice_in_dim(both, core * half, half, 1)
    got = lax.all_gather(mine, "seq", axis=0, tiled=True, axis_index_groups=groups)
    theirs = lax.ppermute(got, "seq", pairs)
    return jnp.where(low_first, jnp.concatenate([got, theirs], 1),
                     jnp.concatenate([theirs, got], 1))


def regroup_weights(attn_in, attn_out, mlp_in, mlp_out, heads_axis, seq_axis):
    rows = attn_in.shape[0]
    model_width = attn_in.shape[2]
    hidden_width = mlp_in.shape[1]
    block_width = model_width // heads_axis
    in_piece = attn_in.astype(jnp.bfloat16).reshape(rows, 3, heads_axis, block_width)
    in_piece = jnp.transpose(in_piece, (0, 2, 1, 3)).reshape(rows, heads_axis, 3 * block_width)
    whole_rows = jnp.concatenate(
        [attn_out.astype(jnp.bfloat16).T, mlp_in.astype(jnp.bfloat16),
         mlp_out.astype(jnp.bfloat16).T], axis=1)
    whole_piece = jnp.broadcast_to(whole_rows[:, None], (rows, heads_axis, whole_rows.shape[1]))
    packed = jnp.concatenate([in_piece, whole_piece], axis=2)
    packed = lax.all_to_all(packed, "head", 1, 0, tiled=True)
    packed = packed.reshape(rows * heads_axis, packed.shape[2])
    in_part = packed[:, :3 * block_width]
    in_part = jnp.broadcast_to(in_part[None], (seq_axis,) + in_part.shape)
    qkv_weight = lax.all_to_all(in_part, "seq", 0, 0, tiled=True)
    qkv_weight = qkv_weight.reshape(-1, 3, block_width)
    early_end = 3 * block_width + model_width + hidden_width
    early = pair_gather(packed[:, 3 * block_width:early_end], seq_axis)
    proj_weight_t = early[:, :model_width]
    up_weight = early[:, model_width:]
    down_weight_t = pair_gather(packed[:, early_end:], seq_axis)
    return qkv_weight, proj_weight_t, up_weight, down_weight_t


def encode_chunk(tokens, lengths, qkv_weight, proj_weight_t, up_weight, down_weight_t,
                 norm_gain, norm_shift, heads_axis, head_index):
    prompts = tokens.shape[0]
    seq_len = tokens.shape[1]
    model_width = tokens.shape[2]
    hidden_width = up_weight.shape[1]
    block_width = model_width // heads_axis
    hidden_block = hidden_width // heads_axis
    local_heads = block_width // DH
    row_count = seq_len // heads_axis
    row_start = head_index * row_count
    projected = jnp.einsum(
        "pld,dte->plte", tokens, qkv_weight, preferred_element_type=jnp.float32
    ).astype(jnp.bfloat16)
    positions = jnp.arange(seq_len, dtype=jnp.int32)
    inside = positions[None, :] < lengths[:, None]
    key_part = projected[:, :, 1]
    value_part = projected[:, :, 2]
    queries = projected[:, :, 0].reshape(prompts, seq_len, local_heads, DH)
    key_heads = key_part.reshape(prompts, seq_len, local_heads, DH)
    value_heads = value_part.reshape(prompts, seq_len, local_heads, DH)
    scores = jnp.einsum(
        "pqhd,pkhd->phqk", queries, key_heads, preferred_element_type=jnp.float32
    ) * (1.0 / math.sqrt(DH))
    scores = jnp.where(inside[:, None, None, :], scores, -1e30)
    row_peak = jnp.max(scores, axis=-1, keepdims=True)
    raised = jnp.exp(scores - row_peak)
    weights = (raised / jnp.sum(raised, axis=-1, keepdims=True)).astype(jnp.bfloat16)
    context = jnp.einsum(
        "phqk,pkhd->pqhd", weights, value_heads, preferred_element_type=jnp.float32
    )
    context = context.astype(jnp.bfloat16).reshape(prompts, heads_axis, row_count, block_width)
    key_cache = jnp.where(inside[:, :, None], key_part, jnp.zeros_like(key_part))
    value_cache = jnp.where(inside[:, :, None], value_part, jnp.zeros_like(value_part))
    context_blocks = jnp.transpose(context, (1, 0, 2, 3))
    context_blocks = lax.all_to_all(context_blocks, "head", 0, 0, tiled=True)
    proj_blocks = proj_weight_t.reshape(model_width, heads_axis, block_width)
    attn_blocks = jnp.einsum(
        "sprf,esf->spre", context_blocks, proj_blocks, preferred_element_type=jnp.float32
    ).astype(jnp.bfloat16)
    attn_rows = jnp.sum(attn_blocks.astype(jnp.float32), axis=0)
    token_rows = lax.dynamic_slice_in_dim(tokens, row_start, row_count, 1)
    normed_rows = layer_norm(
        token_rows.astype(jnp.float32) + attn_rows, norm_gain[0], norm_shift[0]
    ).astype(jnp.bfloat16)
    hidden = jax.nn.gelu(
        jnp.einsum("pld,df->plf", normed_rows, up_weight, preferred_element_type=jnp.float32),
        approximate=False,
    ).astype(jnp.bfloat16)
    hidden = hidden.reshape(prompts, row_count, heads_axis, hidden_block)
    down_blocks = down_weight_t.reshape(model_width, heads_axis, hidden_block)
    mlp_blocks = jnp.einsum(
        "plbf,ebf->plbe", hidden, down_blocks, preferred_element_type=jnp.float32
    ).astype(jnp.bfloat16)
    mlp_rows = jnp.sum(mlp_blocks.astype(jnp.float32), axis=2)
    finished = layer_norm(normed_rows.astype(jnp.float32) + mlp_rows, norm_gain[1], norm_shift[1])
    inside_rows = lax.dynamic_slice_in_dim(inside, row_start, row_count, 1)
    encoded = jnp.where(inside_rows[:, :, None], finished, 0.0).astype(jnp.bfloat16)
    return encoded, key_cache, value_cache


def shards(tokens, lengths, attn_in, attn_out, mlp_in, mlp_out, norm_gain, norm_shift):
    heads_axis = lax.axis_size("head")
    head_index = lax.axis_index("head")
    qkv_weight, proj_weight_t, up_weight, down_weight_t = regroup_weights(
        attn_in, attn_out, mlp_in, mlp_out, heads_axis, lax.axis_size("seq"))
    prompts = tokens.shape[0]
    chunk = max(1, prompts // CHUNKS)
    pieces = []
    for lower in range(0, prompts, chunk):
        pieces.append(encode_chunk(
            tokens[lower:lower + chunk], lengths[lower:lower + chunk], qkv_weight,
            proj_weight_t, up_weight, down_weight_t, norm_gain, norm_shift,
            heads_axis, head_index))
    return tuple(jnp.concatenate(parts, axis=0) for parts in zip(*pieces))


def solution(mesh):
    in_specs = (
        P("seq", None, None),
        P("seq"),
        P(("seq", "head"), None, None),
        P(None, ("seq", "head")),
        P(("seq", "head"), None),
        P(None, ("seq", "head")),
        P(),
        P(),
    )
    out_specs = (P("seq", "head", None), P("seq", None, "head"), P("seq", None, "head"))
    return jax.shard_map(shards, mesh=mesh, in_specs=in_specs, out_specs=out_specs, check_vma=False)
```

```python
import math

import jax
import jax.numpy as jnp
from jax import lax
from jax.sharding import PartitionSpec as P

DH = 64


EPSILON = 1e-05
CHUNKS = 1


def layer_norm(values, gain, shift):
    center = values - jnp.mean(values, axis=-1, keepdims=True)
    spread = jnp.mean(center * center, axis=-1, keepdims=True)
    return center * lax.rsqrt(spread + EPSILON) * gain + shift


def regroup_weights(attn_in, attn_out, mlp_in, mlp_out, heads_axis, seq_axis):
    rows = attn_in.shape[0]
    model_width = attn_in.shape[2]
    hidden_width = mlp_in.shape[1]
    block_width = model_width // heads_axis
    in_piece = attn_in.astype(jnp.bfloat16).reshape(rows, 3, heads_axis, block_width)
    in_piece = jnp.transpose(in_piece, (0, 2, 1, 3)).reshape(rows, heads_axis, 3 * block_width)
    whole_rows = jnp.concatenate(
        [mlp_in.astype(jnp.bfloat16), mlp_out.astype(jnp.bfloat16).T], axis=1)
    whole_piece = jnp.broadcast_to(whole_rows[:, None], (rows, heads_axis, whole_rows.shape[1]))
    packed = jnp.concatenate([in_piece, whole_piece], axis=2)
    packed = lax.all_to_all(packed, "head", 1, 0, tiled=True)
    packed = packed.reshape(rows * heads_axis, packed.shape[2])
    in_part = packed[:, :3 * block_width]
    in_part = jnp.broadcast_to(in_part[None], (seq_axis,) + in_part.shape)
    qkv_weight = lax.all_to_all(in_part, "seq", 0, 0, tiled=True)
    qkv_weight = qkv_weight.reshape(-1, 3, block_width)
    up_end = 3 * block_width + hidden_width
    up_weight = lax.all_gather(packed[:, 3 * block_width:up_end], "seq", axis=0, tiled=True)
    down_weight_t = lax.all_gather(packed[:, up_end:], "seq", axis=0, tiled=True)
    out_rows = attn_out.astype(jnp.bfloat16).T
    out_rows = jnp.broadcast_to(out_rows[None], (seq_axis,) + out_rows.shape)
    out_rows = lax.all_to_all(out_rows, "seq", 0, 0, tiled=True)
    out_rows = jnp.broadcast_to(out_rows[None], (heads_axis,) + out_rows.shape)
    out_rows = lax.all_to_all(out_rows, "head", 0, 0, tiled=True)
    proj_weight_t = jnp.transpose(out_rows, (1, 0, 2, 3)).reshape(-1, model_width)
    return qkv_weight, proj_weight_t, up_weight, down_weight_t


def encode_chunk(tokens, lengths, qkv_weight, proj_weight_t, up_weight, down_weight_t,
                 norm_gain, norm_shift, heads_axis, head_index):
    prompts = tokens.shape[0]
    seq_len = tokens.shape[1]
    model_width = tokens.shape[2]
    hidden_width = up_weight.shape[1]
    block_width = model_width // heads_axis
    hidden_block = hidden_width // heads_axis
    local_heads = block_width // DH
    row_count = seq_len // heads_axis
    row_start = head_index * row_count
    projected = jnp.einsum(
        "pld,dte->plte", tokens, qkv_weight, preferred_element_type=jnp.float32
    ).astype(jnp.bfloat16)
    positions = jnp.arange(seq_len, dtype=jnp.int32)
    inside = positions[None, :] < lengths[:, None]
    key_part = projected[:, :, 1]
    value_part = projected[:, :, 2]
    queries = projected[:, :, 0].reshape(prompts, seq_len, local_heads, DH)
    key_heads = key_part.reshape(prompts, seq_len, local_heads, DH)
    value_heads = value_part.reshape(prompts, seq_len, local_heads, DH)
    scores = jnp.einsum(
        "pqhd,pkhd->phqk", queries, key_heads, preferred_element_type=jnp.float32
    ) * (1.0 / math.sqrt(DH))
    scores = jnp.where(inside[:, None, None, :], scores, -1e30)
    row_peak = jnp.max(scores, axis=-1, keepdims=True)
    raised = jnp.exp(scores - row_peak)
    weights = (raised / jnp.sum(raised, axis=-1, keepdims=True)).astype(jnp.bfloat16)
    context = jnp.einsum(
        "phqk,pkhd->pqhd", weights, value_heads, preferred_element_type=jnp.float32
    )
    context = context.astype(jnp.bfloat16).reshape(prompts, heads_axis, row_count, block_width)
    key_cache = jnp.where(inside[:, :, None], key_part, jnp.zeros_like(key_part))
    value_cache = jnp.where(inside[:, :, None], value_part, jnp.zeros_like(value_part))
    context_blocks = jnp.transpose(context, (1, 0, 2, 3))
    context_blocks = lax.all_to_all(context_blocks, "head", 0, 0, tiled=True)
    proj_blocks = proj_weight_t.reshape(model_width, heads_axis, block_width)
    attn_blocks = jnp.einsum(
        "sprf,esf->spre", context_blocks, proj_blocks, preferred_element_type=jnp.float32
    ).astype(jnp.bfloat16)
    attn_rows = jnp.sum(attn_blocks.astype(jnp.float32), axis=0)
    token_rows = lax.dynamic_slice_in_dim(tokens, row_start, row_count, 1)
    normed_rows = layer_norm(
        token_rows.astype(jnp.float32) + attn_rows, norm_gain[0], norm_shift[0]
    ).astype(jnp.bfloat16)
    hidden = jax.nn.gelu(
        jnp.einsum("pld,df->plf", normed_rows, up_weight, preferred_element_type=jnp.float32),
        approximate=False,
    ).astype(jnp.bfloat16)
    hidden = hidden.reshape(prompts, row_count, heads_axis, hidden_block)
    down_blocks = down_weight_t.reshape(model_width, heads_axis, hidden_block)
    mlp_blocks = jnp.einsum(
        "plbf,ebf->plbe", hidden, down_blocks, preferred_element_type=jnp.float32
    ).astype(jnp.bfloat16)
    mlp_rows = jnp.sum(mlp_blocks.astype(jnp.float32), axis=2)
    finished = layer_norm(normed_rows.astype(jnp.float32) + mlp_rows, norm_gain[1], norm_shift[1])
    inside_rows = lax.dynamic_slice_in_dim(inside, row_start, row_count, 1)
    encoded = jnp.where(inside_rows[:, :, None], finished, 0.0).astype(jnp.bfloat16)
    return encoded, key_cache, value_cache


def shards(tokens, lengths, attn_in, attn_out, mlp_in, mlp_out, norm_gain, norm_shift):
    heads_axis = lax.axis_size("head")
    head_index = lax.axis_index("head")
    qkv_weight, proj_weight_t, up_weight, down_weight_t = regroup_weights(
        attn_in, attn_out, mlp_in, mlp_out, heads_axis, lax.axis_size("seq"))
    prompts = tokens.shape[0]
    chunk = max(1, prompts // CHUNKS)
    pieces = []
    for lower in range(0, prompts, chunk):
        pieces.append(encode_chunk(
            tokens[lower:lower + chunk], lengths[lower:lower + chunk], qkv_weight,
            proj_weight_t, up_weight, down_weight_t, norm_gain, norm_shift,
            heads_axis, head_index))
    return tuple(jnp.concatenate(parts, axis=0) for parts in zip(*pieces))


def solution(mesh):
    in_specs = (
        P("seq", None, None),
        P("seq"),
        P(("seq", "head"), None, None),
        P(None, ("seq", "head")),
        P(("seq", "head"), None),
        P(None, ("seq", "head")),
        P(),
        P(),
    )
    out_specs = (P("seq", "head", None), P("seq", None, "head"), P("seq", None, "head"))
    return jax.shard_map(shards, mesh=mesh, in_specs=in_specs, out_specs=out_specs, check_vma=False)
```

```python
import math

import jax
import jax.numpy as jnp
from jax import lax
from jax.sharding import PartitionSpec as P

DH = 64


EPSILON = 1e-05
CHUNKS = 1


def layer_norm(values, gain, shift):
    center = values - jnp.mean(values, axis=-1, keepdims=True)
    spread = jnp.mean(center * center, axis=-1, keepdims=True)
    return center * lax.rsqrt(spread + EPSILON) * gain + shift


def regroup_weights(attn_in, attn_out, mlp_in, mlp_out, heads_axis, seq_axis):
    rows = attn_in.shape[0]
    model_width = attn_in.shape[2]
    hidden_width = mlp_in.shape[1]
    block_width = model_width // heads_axis
    in_piece = attn_in.astype(jnp.bfloat16).reshape(rows, 3, heads_axis, block_width)
    in_piece = jnp.transpose(in_piece, (0, 2, 1, 3)).reshape(rows, heads_axis, 3 * block_width)
    whole_rows = jnp.concatenate(
        [attn_out.astype(jnp.bfloat16).T, mlp_in.astype(jnp.bfloat16),
         mlp_out.astype(jnp.bfloat16).T], axis=1)
    whole_piece = jnp.broadcast_to(whole_rows[:, None], (rows, heads_axis, whole_rows.shape[1]))
    packed = jnp.concatenate([in_piece, whole_piece], axis=2)
    packed = lax.all_to_all(packed, "head", 1, 0, tiled=True)
    packed = packed.reshape(rows * heads_axis, packed.shape[2])
    in_part = packed[:, :3 * block_width]
    in_part = jnp.broadcast_to(in_part[None], (seq_axis,) + in_part.shape)
    qkv_weight = lax.all_to_all(in_part, "seq", 0, 0, tiled=True)
    qkv_weight = qkv_weight.reshape(-1, 3, block_width)
    early_end = 3 * block_width + model_width + hidden_width
    early = lax.all_gather(packed[:, 3 * block_width:early_end], "seq", axis=0, tiled=True)
    proj_weight_t = early[:, :model_width]
    up_weight = early[:, model_width:]
    down_weight_t = lax.all_gather(packed[:, early_end:], "seq", axis=0, tiled=True)
    return qkv_weight, proj_weight_t, up_weight, down_weight_t


def encode_chunk(tokens, lengths, qkv_weight, proj_weight_t, up_weight, down_weight_t,
                 norm_gain, norm_shift, heads_axis, head_index):
    prompts = tokens.shape[0]
    seq_len = tokens.shape[1]
    model_width = tokens.shape[2]
    hidden_width = up_weight.shape[1]
    block_width = model_width // heads_axis
    hidden_block = hidden_width // heads_axis
    local_heads = block_width // DH
    row_count = seq_len // heads_axis
    row_start = head_index * row_count
    projected = jnp.einsum(
        "pld,dte->plte", tokens, qkv_weight, preferred_element_type=jnp.float32
    ).astype(jnp.bfloat16)
    positions = jnp.arange(seq_len, dtype=jnp.int32)
    inside = positions[None, :] < lengths[:, None]
    key_part = projected[:, :, 1]
    value_part = projected[:, :, 2]
    queries = projected[:, :, 0].reshape(prompts, seq_len, local_heads, DH)
    key_heads = key_part.reshape(prompts, seq_len, local_heads, DH)
    value_heads = value_part.reshape(prompts, seq_len, local_heads, DH)
    scores = jnp.einsum(
        "pqhd,pkhd->phqk", queries, key_heads, preferred_element_type=jnp.float32
    ) * (1.0 / math.sqrt(DH))
    scores = jnp.where(inside[:, None, None, :], scores, -1e30)
    row_peak = jnp.max(scores, axis=-1, keepdims=True)
    raised = jnp.exp(scores - row_peak)
    weights = (raised / jnp.sum(raised, axis=-1, keepdims=True)).astype(jnp.bfloat16)
    context = jnp.einsum(
        "phqk,pkhd->pqhd", weights, value_heads, preferred_element_type=jnp.float32
    )
    context = context.astype(jnp.bfloat16).reshape(prompts, heads_axis, row_count, block_width)
    key_cache = jnp.where(inside[:, :, None], key_part, jnp.zeros_like(key_part))
    value_cache = jnp.where(inside[:, :, None], value_part, jnp.zeros_like(value_part))
    context_blocks = jnp.transpose(context, (1, 0, 2, 3))
    context_blocks = lax.all_to_all(context_blocks, "head", 0, 0, tiled=True)
    proj_blocks = proj_weight_t.reshape(model_width, heads_axis, block_width)
    attn_rows = jnp.einsum(
        "sprf,esf->pre", context_blocks, proj_blocks, preferred_element_type=jnp.float32)
    token_rows = lax.dynamic_slice_in_dim(tokens, row_start, row_count, 1)
    normed_rows = layer_norm(
        token_rows.astype(jnp.float32) + attn_rows, norm_gain[0], norm_shift[0]
    ).astype(jnp.bfloat16)
    hidden = jax.nn.gelu(
        jnp.einsum("pld,df->plf", normed_rows, up_weight, preferred_element_type=jnp.float32),
        approximate=False,
    ).astype(jnp.bfloat16)
    mlp_rows = jnp.einsum(
        "plf,ef->ple", hidden, down_weight_t, preferred_element_type=jnp.float32)
    finished = layer_norm(normed_rows.astype(jnp.float32) + mlp_rows, norm_gain[1], norm_shift[1])
    inside_rows = lax.dynamic_slice_in_dim(inside, row_start, row_count, 1)
    encoded = jnp.where(inside_rows[:, :, None], finished, 0.0).astype(jnp.bfloat16)
    return encoded, key_cache, value_cache


def shards(tokens, lengths, attn_in, attn_out, mlp_in, mlp_out, norm_gain, norm_shift):
    heads_axis = lax.axis_size("head")
    head_index = lax.axis_index("head")
    qkv_weight, proj_weight_t, up_weight, down_weight_t = regroup_weights(
        attn_in, attn_out, mlp_in, mlp_out, heads_axis, lax.axis_size("seq"))
    prompts = tokens.shape[0]
    chunk = max(1, prompts // CHUNKS)
    pieces = []
    for lower in range(0, prompts, chunk):
        pieces.append(encode_chunk(
            tokens[lower:lower + chunk], lengths[lower:lower + chunk], qkv_weight,
            proj_weight_t, up_weight, down_weight_t, norm_gain, norm_shift,
            heads_axis, head_index))
    return tuple(jnp.concatenate(parts, axis=0) for parts in zip(*pieces))


def solution(mesh):
    in_specs = (
        P("seq", None, None),
        P("seq"),
        P(("seq", "head"), None, None),
        P(None, ("seq", "head")),
        P(("seq", "head"), None),
        P(None, ("seq", "head")),
        P(),
        P(),
    )
    out_specs = (P("seq", "head", None), P("seq", None, "head"), P("seq", None, "head"))
    return jax.shard_map(shards, mesh=mesh, in_specs=in_specs, out_specs=out_specs, check_vma=False)
```

```python
import math

import jax
import jax.numpy as jnp
from jax import lax
from jax.sharding import PartitionSpec as P

DH = 64


EPSILON = 1e-05
CHUNKS = 1


def layer_norm(values, gain, shift):
    center = values - jnp.mean(values, axis=-1, keepdims=True)
    spread = jnp.mean(center * center, axis=-1, keepdims=True)
    return center * lax.rsqrt(spread + EPSILON) * gain + shift


def regroup_weights(attn_in, attn_out, mlp_in, mlp_out, heads_axis, seq_axis):
    rows = attn_in.shape[0]
    model_width = attn_in.shape[2]
    hidden_width = mlp_in.shape[1]
    block_width = model_width // heads_axis
    in_piece = attn_in.astype(jnp.bfloat16).reshape(rows, 3, heads_axis, block_width)
    in_piece = jnp.transpose(in_piece, (0, 2, 1, 3)).reshape(rows, heads_axis, 3 * block_width)
    whole_rows = jnp.concatenate(
        [attn_out.astype(jnp.bfloat16).T, mlp_in.astype(jnp.bfloat16),
         mlp_out.astype(jnp.bfloat16).T], axis=1)
    whole_piece = jnp.broadcast_to(whole_rows[:, None], (rows, heads_axis, whole_rows.shape[1]))
    packed = jnp.concatenate([in_piece, whole_piece], axis=2)
    packed = lax.all_to_all(packed, "head", 1, 0, tiled=True)
    packed = packed.reshape(rows * heads_axis, packed.shape[2])
    in_part = packed[:, :3 * block_width]
    in_part = jnp.broadcast_to(in_part[None], (seq_axis,) + in_part.shape)
    qkv_weight = lax.all_to_all(in_part, "seq", 0, 0, tiled=True)
    qkv_weight = qkv_weight.reshape(-1, 3, block_width)
    early_end = 3 * block_width + model_width + hidden_width
    early = lax.all_gather(packed[:, 3 * block_width:early_end], "seq", axis=0, tiled=True)
    proj_weight_t = early[:, :model_width]
    up_weight = early[:, model_width:]
    down_weight_t = lax.all_gather(packed[:, early_end:], "seq", axis=0, tiled=True)
    return qkv_weight, proj_weight_t, up_weight, down_weight_t


def encode_chunk(tokens, lengths, qkv_weight, proj_weight_t, up_weight, down_weight_t,
                 norm_gain, norm_shift, heads_axis, head_index):
    prompts = tokens.shape[0]
    seq_len = tokens.shape[1]
    model_width = tokens.shape[2]
    hidden_width = up_weight.shape[1]
    block_width = model_width // heads_axis
    hidden_block = hidden_width // heads_axis
    local_heads = block_width // DH
    row_count = seq_len // heads_axis
    row_start = head_index * row_count
    projected = jnp.einsum(
        "pld,dte->plte", tokens, qkv_weight, preferred_element_type=jnp.float32
    ).astype(jnp.bfloat16)
    positions = jnp.arange(seq_len, dtype=jnp.int32)
    inside = positions[None, :] < lengths[:, None]
    key_part = projected[:, :, 1]
    value_part = projected[:, :, 2]
    queries = projected[:, :, 0].reshape(prompts, seq_len, local_heads, DH)
    key_heads = key_part.reshape(prompts, seq_len, local_heads, DH)
    value_heads = value_part.reshape(prompts, seq_len, local_heads, DH)
    scores = jnp.einsum(
        "pqhd,pkhd->phqk", queries, key_heads, preferred_element_type=jnp.float32
    ) * (1.0 / math.sqrt(DH))
    scores = jnp.where(inside[:, None, None, :], scores, -1e30)
    row_peak = jnp.max(scores, axis=-1, keepdims=True)
    raised = jnp.exp(scores - row_peak)
    weights = (raised / jnp.sum(raised, axis=-1, keepdims=True)).astype(jnp.bfloat16)
    context = jnp.einsum(
        "phqk,pkhd->pqhd", weights, value_heads, preferred_element_type=jnp.float32
    )
    context = context.astype(jnp.bfloat16).reshape(prompts, heads_axis, row_count, block_width)
    key_cache = jnp.where(inside[:, :, None], key_part, jnp.zeros_like(key_part))
    value_cache = jnp.where(inside[:, :, None], value_part, jnp.zeros_like(value_part))
    context_blocks = jnp.transpose(context, (1, 0, 2, 3))
    context_blocks = lax.all_to_all(context_blocks, "head", 0, 0, tiled=True)
    proj_blocks = proj_weight_t.reshape(model_width, heads_axis, block_width)
    attn_blocks = jnp.einsum(
        "sprf,esf->spre", context_blocks, proj_blocks, preferred_element_type=jnp.float32
    ).astype(jnp.bfloat16)
    attn_rows = jnp.sum(attn_blocks.astype(jnp.float32), axis=0)
    token_rows = lax.dynamic_slice_in_dim(tokens, row_start, row_count, 1)
    normed_rows = layer_norm(
        token_rows.astype(jnp.float32) + attn_rows, norm_gain[0], norm_shift[0]
    ).astype(jnp.bfloat16)
    hidden = jax.nn.gelu(
        jnp.einsum("pld,df->plf", normed_rows, up_weight, preferred_element_type=jnp.float32),
        approximate=False,
    ).astype(jnp.bfloat16)
    hidden = lax.optimization_barrier(hidden)
    mlp_rows = jnp.einsum(
        "plf,ef->ple", hidden, down_weight_t, preferred_element_type=jnp.float32)
    finished = layer_norm(normed_rows.astype(jnp.float32) + mlp_rows, norm_gain[1], norm_shift[1])
    inside_rows = lax.dynamic_slice_in_dim(inside, row_start, row_count, 1)
    encoded = jnp.where(inside_rows[:, :, None], finished, 0.0).astype(jnp.bfloat16)
    return encoded, key_cache, value_cache


def shards(tokens, lengths, attn_in, attn_out, mlp_in, mlp_out, norm_gain, norm_shift):
    heads_axis = lax.axis_size("head")
    head_index = lax.axis_index("head")
    qkv_weight, proj_weight_t, up_weight, down_weight_t = regroup_weights(
        attn_in, attn_out, mlp_in, mlp_out, heads_axis, lax.axis_size("seq"))
    prompts = tokens.shape[0]
    chunk = max(1, prompts // CHUNKS)
    pieces = []
    for lower in range(0, prompts, chunk):
        pieces.append(encode_chunk(
            tokens[lower:lower + chunk], lengths[lower:lower + chunk], qkv_weight,
            proj_weight_t, up_weight, down_weight_t, norm_gain, norm_shift,
            heads_axis, head_index))
    return tuple(jnp.concatenate(parts, axis=0) for parts in zip(*pieces))


def solution(mesh):
    in_specs = (
        P("seq", None, None),
        P("seq"),
        P(("seq", "head"), None, None),
        P(None, ("seq", "head")),
        P(("seq", "head"), None),
        P(None, ("seq", "head")),
        P(),
        P(),
    )
    out_specs = (P("seq", "head", None), P("seq", None, "head"), P("seq", None, "head"))
    return jax.shard_map(shards, mesh=mesh, in_specs=in_specs, out_specs=out_specs, check_vma=False)
```

```python
import math

import jax
import jax.numpy as jnp
from jax import lax
from jax.sharding import PartitionSpec as P

DH = 64


EPSILON = 1e-05
CHUNKS = 1


def layer_norm(values, gain, shift):
    center = values - jnp.mean(values, axis=-1, keepdims=True)
    spread = jnp.mean(center * center, axis=-1, keepdims=True)
    return center * lax.rsqrt(spread + EPSILON) * gain + shift


def regroup_weights(attn_in, attn_out, mlp_in, mlp_out, heads_axis, seq_axis):
    rows = attn_in.shape[0]
    model_width = attn_in.shape[2]
    hidden_width = mlp_in.shape[1]
    block_width = model_width // heads_axis
    in_piece = attn_in.astype(jnp.bfloat16).reshape(rows, 3, heads_axis, block_width)
    in_piece = jnp.transpose(in_piece, (0, 2, 1, 3)).reshape(rows, heads_axis, 3 * block_width)
    whole_rows = jnp.concatenate(
        [attn_out.astype(jnp.bfloat16).T, mlp_in.astype(jnp.bfloat16),
         mlp_out.astype(jnp.bfloat16).T], axis=1)
    whole_piece = jnp.broadcast_to(whole_rows[:, None], (rows, heads_axis, whole_rows.shape[1]))
    packed = jnp.concatenate([in_piece, whole_piece], axis=2)
    packed = lax.all_to_all(packed, "head", 1, 0, tiled=True)
    packed = packed.reshape(rows * heads_axis, packed.shape[2])
    in_part = packed[:, :3 * block_width]
    in_part = jnp.broadcast_to(in_part[None], (seq_axis,) + in_part.shape)
    qkv_weight = lax.all_to_all(in_part, "seq", 0, 0, tiled=True)
    qkv_weight = qkv_weight.reshape(-1, 3, block_width)
    early_end = 3 * block_width + model_width + hidden_width
    early = lax.all_gather(packed[:, 3 * block_width:early_end], "seq", axis=0, tiled=True)
    proj_weight_t = early[:, :model_width]
    up_weight = early[:, model_width:]
    down_weight_t = lax.all_gather(packed[:, early_end:], "seq", axis=0, tiled=True)
    return qkv_weight, proj_weight_t, up_weight, down_weight_t


def encode_chunk(tokens, lengths, qkv_weight, proj_weight_t, up_weight, down_weight_t,
                 norm_gain, norm_shift, heads_axis, head_index):
    prompts = tokens.shape[0]
    seq_len = tokens.shape[1]
    model_width = tokens.shape[2]
    hidden_width = up_weight.shape[1]
    block_width = model_width // heads_axis
    hidden_block = hidden_width // heads_axis
    local_heads = block_width // DH
    row_count = seq_len // heads_axis
    row_start = head_index * row_count
    projected = jnp.einsum(
        "pld,dte->plte", tokens, qkv_weight, preferred_element_type=jnp.float32
    ).astype(jnp.bfloat16)
    positions = jnp.arange(seq_len, dtype=jnp.int32)
    inside = positions[None, :] < lengths[:, None]
    key_part = projected[:, :, 1]
    value_part = projected[:, :, 2]
    queries = projected[:, :, 0].reshape(prompts, seq_len, local_heads, DH)
    key_heads = key_part.reshape(prompts, seq_len, local_heads, DH)
    value_heads = value_part.reshape(prompts, seq_len, local_heads, DH)
    scores = jnp.einsum(
        "pqhd,pkhd->phqk", queries, key_heads, preferred_element_type=jnp.float32
    ) * (1.0 / math.sqrt(DH))
    scores = jnp.where(inside[:, None, None, :], scores, -1e30)
    row_peak = jnp.max(scores, axis=-1, keepdims=True)
    raised = jnp.exp(scores - row_peak)
    weights = (raised / jnp.sum(raised, axis=-1, keepdims=True)).astype(jnp.bfloat16)
    context = jnp.einsum(
        "phqk,pkhd->pqhd", weights, value_heads, preferred_element_type=jnp.float32
    )
    context = context.astype(jnp.bfloat16).reshape(prompts, heads_axis, row_count, block_width)
    key_cache = jnp.where(inside[:, :, None], key_part, jnp.zeros_like(key_part))
    value_cache = jnp.where(inside[:, :, None], value_part, jnp.zeros_like(value_part))
    context_blocks = jnp.transpose(context, (1, 0, 2, 3))
    context_blocks = lax.all_to_all(context_blocks, "head", 0, 0, tiled=True)
    proj_blocks = proj_weight_t.reshape(model_width, heads_axis, block_width)
    attn_rows = jnp.einsum(
        "sprf,esf->pre", context_blocks, proj_blocks, preferred_element_type=jnp.float32)
    token_rows = lax.dynamic_slice_in_dim(tokens, row_start, row_count, 1)
    normed_rows = layer_norm(
        token_rows.astype(jnp.float32) + attn_rows, norm_gain[0], norm_shift[0]
    ).astype(jnp.bfloat16)
    hidden = jax.nn.gelu(
        jnp.einsum("pld,df->plf", normed_rows, up_weight, preferred_element_type=jnp.float32),
        approximate=False,
    ).astype(jnp.bfloat16)
    hidden = lax.optimization_barrier(hidden)
    mlp_rows = jnp.einsum(
        "plf,ef->ple", hidden, down_weight_t, preferred_element_type=jnp.float32)
    finished = layer_norm(normed_rows.astype(jnp.float32) + mlp_rows, norm_gain[1], norm_shift[1])
    inside_rows = lax.dynamic_slice_in_dim(inside, row_start, row_count, 1)
    encoded = jnp.where(inside_rows[:, :, None], finished, 0.0).astype(jnp.bfloat16)
    return encoded, key_cache, value_cache


def shards(tokens, lengths, attn_in, attn_out, mlp_in, mlp_out, norm_gain, norm_shift):
    heads_axis = lax.axis_size("head")
    head_index = lax.axis_index("head")
    qkv_weight, proj_weight_t, up_weight, down_weight_t = regroup_weights(
        attn_in, attn_out, mlp_in, mlp_out, heads_axis, lax.axis_size("seq"))
    prompts = tokens.shape[0]
    chunk = max(1, prompts // CHUNKS)
    pieces = []
    for lower in range(0, prompts, chunk):
        pieces.append(encode_chunk(
            tokens[lower:lower + chunk], lengths[lower:lower + chunk], qkv_weight,
            proj_weight_t, up_weight, down_weight_t, norm_gain, norm_shift,
            heads_axis, head_index))
    return tuple(jnp.concatenate(parts, axis=0) for parts in zip(*pieces))


def solution(mesh):
    in_specs = (
        P("seq", None, None),
        P("seq"),
        P(("seq", "head"), None, None),
        P(None, ("seq", "head")),
        P(("seq", "head"), None),
        P(None, ("seq", "head")),
        P(),
        P(),
    )
    out_specs = (P("seq", "head", None), P("seq", None, "head"), P("seq", None, "head"))
    return jax.shard_map(shards, mesh=mesh, in_specs=in_specs, out_specs=out_specs, check_vma=False)
```
